128 devices in a mesh: grp: 2 (over core), gx: 32 (over z_hi, y, x), gy: 2 (over z_lo).
Axes of the slice: x: 4, y: 4, z: 4 (z_hi: 2, z_lo: 2; z = z_hi * 2 + z_lo), core: 2. Of those that a mesh axis runs over, the one named last changes fastest.
Arguments:
- les_velocity: float32 [1024, 32, 3, 512], P('gx', 'gy', None, 'grp'), may hold values from -6 to 6
- mean_mach: float32 [512, 32], P('gx', 'gy'), may hold values from 0.2 to 0.6
- transfer_tiles: bfloat16 [256, 2, 2, 64, 64], P('gx', 'gy'), may hold values from -0.75 to 0.75
- intersection_offset: int32 [256], P('gx'), may hold values from -1 to 1, as said below
- acoustic_state: float32 [512, 32, 4, 512], P('gx', 'gy', None, 'grp'), may hold values from -6 to 6
Outputs:
- acoustic_out: float32 [512, 32, 4, 512], P('gx', 'gy', None, 'grp')
The draws below stay inside these ranges and needn't reach their ends.
Inputs may be any that keep to these rules, and one draw needn't show every extreme that they name: `intersection_offset`: each value is -1 or 1. The first block of every gx shard has -1 and the last has 1, except that the first two blocks of the grid have 1 and the last two have -1.
All inputs are finite; a program needn't handle non-finite values.
Results may differ from the reference program's by a relative error of at most 0.018.
Values sent between devices are 32-bit elements; how exact they have to be, the bound alone decides.
A program may use at most 128 MiB of HBM per device.

```python
import jax
import jax.numpy as jnp
from jax import lax

CYL = 16
STEPS = 2
NBL = 8
PLANE = 64
NXL = 1024
NXA = 512
NY = 32
NZ = 512
NBX = 256
NBXA = 128
N_GY = 2


def draw_intersection_offset(key, part):
    coins = jax.random.randint(key, (NBX,), 0, 2).astype(jnp.int32) * 2 - 1
    position = jnp.arange(NBX, dtype=jnp.int32)
    local = position % NBL
    offsets = jnp.where(local == 0, -1, jnp.where(local == NBL - 1, 1, coins))
    offsets = jnp.where(position < 2, 1, jnp.where(position >= NBX - 2, -1, offsets))
    return offsets.astype(jnp.int32)


def draw_acoustic_state(key, part):
    shape = (NXA, NY, 4, NZ)
    values = jax.random.normal(key, shape, jnp.float32)
    return jnp.clip(values, -6.0, 6.0).astype(jnp.float32)


def block_scale(key, dims, pieces, smallest, top_value):
    def one(axis_at, parts):
        heights = jax.random.uniform(jax.random.fold_in(jax.random.fold_in(key, 6), axis_at), (parts,), jnp.float32, smallest / len(pieces), top_value / len(pieces))
        return jnp.repeat(jnp.exp(heights), dims[axis_at] // parts).reshape((-1,) + (1,) * (len(dims) - axis_at - 1))

    level = one(*pieces[0])
    for cut in pieces[1:]:
        level = level * one(*cut)
    return level


def normal_values(key, extent, scale, most, split=(), kind=jnp.bfloat16):
    result = scale * jax.random.normal(key, extent, jnp.float32)
    if split:
        result = result * block_scale(key, extent, split, -0.22, 0.18)
    return jnp.clip(result, -most, most).astype(kind)


def setup_inputs(seed: int = 0) -> dict:
    arg_keys = jax.random.split(jax.random.key(seed), 6)
    les_velocity = normal_values(arg_keys[0], (NXL, NY, 3, NZ), 1.0, 6.0, ((0, 32), (1, 2), (3, 2)), jnp.float32)
    mean_mach = jnp.clip(0.2 + 0.400000021 * jax.random.uniform(arg_keys[1], (NXA, NY), jnp.float32) ** block_scale(arg_keys[1], (NXA, NY), ((0, 32), (1, 2)), -0.2, 0.2), 0.2, 0.6)
    transfer_tiles = normal_values(arg_keys[2], (NBX, N_GY, 2, PLANE, PLANE), PLANE ** -0.5, 0.75, ((0, 32), (1, 2)))
    intersection_offset = draw_intersection_offset(jax.random.fold_in(arg_keys[5], 71), 0)
    acoustic_state = draw_acoustic_state(jax.random.fold_in(arg_keys[5], 71), 0)
    return dict(les_velocity=les_velocity, mean_mach=mean_mach, transfer_tiles=transfer_tiles, intersection_offset=intersection_offset, acoustic_state=acoustic_state)


eddy_step = 0.1
viscosity = 0.5
wave_step = 0.2
filter_weight = 0.2
derivative_weights = (0.770882380518, -0.166705904415, 0.020843142770)
filter_taps = (0.287392842460, -0.226146951809, 0.106303578770, -0.023853048191)
unit_moves = ((1, 0, 0), (0, 1, 0), (0, 0, 1))


def window(array, along_x, along_y, along_z, margin):
    return array[margin + along_x: array.shape[0] - margin + along_x,
                 margin + along_y: array.shape[1] - margin + along_y, :,
                 margin + along_z: array.shape[3] - margin + along_z]


def les_terms(padded):
    center = window(padded, 0, 0, 0, 1)
    grads = []
    laplace = -6.0 * center
    for move in unit_moves:
        ahead = window(padded, move[0], move[1], move[2], 1)
        behind = window(padded, -move[0], -move[1], -move[2], 1)
        grads.append(0.5 * (ahead - behind))
        laplace = laplace + ahead + behind
    vort_x = grads[1][:, :, 2] - grads[2][:, :, 1]
    vort_y = grads[2][:, :, 0] - grads[0][:, :, 2]
    vort_z = grads[0][:, :, 1] - grads[1][:, :, 0]
    lamb = jnp.stack([vort_y * center[:, :, 2] - vort_z * center[:, :, 1],
                      vort_z * center[:, :, 0] - vort_x * center[:, :, 2],
                      vort_x * center[:, :, 1] - vort_y * center[:, :, 0]], axis=2)
    return lamb, laplace


def derivative(padded, move):
    total = None
    for index in range(3):
        reach = index + 1
        ahead = window(padded, reach * move[0], reach * move[1], reach * move[2], 3)
        behind = window(padded, -reach * move[0], -reach * move[1], -reach * move[2], 3)
        term = derivative_weights[index] * (ahead - behind)
        total = term if total is None else total + term
    return total


def rate(padded, mach, source):
    grads = [derivative(padded, move) for move in unit_moves]
    convect = mach[:, :, None, None] * grads[0]
    pressure_rate = -(convect[:, :, 0] + grads[0][:, :, 1] + grads[1][:, :, 2] + grads[2][:, :, 3])
    x_rate = -(convect[:, :, 1] + grads[0][:, :, 0]) - source[:, :, 0]
    y_rate = -(convect[:, :, 2] + grads[1][:, :, 0]) - source[:, :, 1]
    z_rate = -(convect[:, :, 3] + grads[2][:, :, 0]) - source[:, :, 2]
    return jnp.stack([pressure_rate, x_rate, y_rate, z_rate], axis=2)


def smooth(padded):
    center = window(padded, 0, 0, 0, 3)
    total = 3.0 * filter_taps[0] * center
    for move in unit_moves:
        for index in range(1, 4):
            ahead = window(padded, index * move[0], index * move[1], index * move[2], 3)
            behind = window(padded, -index * move[0], -index * move[1], -index * move[2], 3)
            total = total + filter_taps[index] * (ahead + behind)
    return center - filter_weight * total


def pad_three(state):
    return jnp.pad(state, ((3, 3), (3, 3), (0, 0), (3, 3)))


def restrict(source, tiles, offsets):
    depth = source.shape[3]
    target = (jnp.arange(NBX, dtype=jnp.int32) // 2 + offsets).astype(jnp.int32)
    slabs = []
    for slab in range(N_GY):
        part = source[:, slab * CYL:(slab + 1) * CYL]
        blocks = part.reshape(NBX, PLANE, 3 * depth)
        terms = jnp.einsum('bkpq,bpc->bkqc', tiles[:, slab].astype(jnp.float32), blocks.astype(jnp.float32),
                           precision=lax.Precision.HIGHEST)
        bricks = terms[:, 0].reshape(NBXA, 2, PLANE, 3 * depth).sum(axis=1)
        bricks = bricks.at[target].add(terms[:, 1])
        slabs.append(bricks.reshape(NXA, CYL, 3, depth))
    return jnp.concatenate(slabs, axis=1)


def reference(les_velocity, mean_mach, transfer_tiles, intersection_offset, acoustic_state):
    velocity = les_velocity
    sources = []
    for step in range(STEPS):
        lamb, laplace = les_terms(jnp.pad(velocity, ((1, 1), (1, 1), (0, 0), (1, 1))))
        sources.append(restrict(lamb, transfer_tiles, intersection_offset))
        if step + 1 < STEPS:
            velocity = velocity + eddy_step * (viscosity * laplace - lamb)
    state = acoustic_state
    for source in sources:
        first = rate(pad_three(state), mean_mach, source)
        middle = state + wave_step * first
        second = rate(pad_three(middle), mean_mach, source)
        updated = state + 0.5 * wave_step * (first + second)
        state = smooth(pad_three(updated))
    return state
```

```python
import functools

import jax
import jax.numpy as jnp
from jax import lax
from jax.experimental import pallas as pl
from jax.experimental.pallas import tpu as pltpu
from jax.sharding import PartitionSpec as P

MESH = pl.DeviceIdType.MESH
F32, BF16 = jnp.float32, jnp.bfloat16

eddy_step = 0.1
viscosity = 0.5
wave_step = 0.2
filter_weight = 0.2
derivative_weights = (0.770882380518, -0.166705904415, 0.02084314277)
filter_taps = (0.28739284246, -0.226146951809, 0.10630357877, -0.023853048191)

NX, NA, NY, L = 32, 16, 16, 128
R0 = 8
EX = 3
STAGES = 6
ROWS = pl.ds(R0, NY)


def kernel(count, les, mach, tiles, offs, state, out, v0, v1, zv, f, zf, stage, lb, wk, s, tb, mb, tl, mc,
           send, recv, local):
    ix, iy, ig = lax.axis_index("gx"), lax.axis_index("gy"), lax.axis_index("grp")
    has_l, has_r = ix > 0, ix < count - 1
    right = {"gx": jnp.minimum(ix + 1, count - 1)}
    left = {"gx": jnp.maximum(ix - 1, 0)}
    side, twin = {"gy": 1 - iy}, {"grp": 1 - ig}

    loads = []
    for h in range(2):
        loads.append(pltpu.make_async_copy(les.at[:, :, :, pl.ds(L * h, L)], v0.at[pl.ds(1, NX), :, h, ROWS, :], local.at[h]))
    loads.append(pltpu.make_async_copy(state, stage, local.at[2]))
    loads.append(pltpu.make_async_copy(tiles, tl, local.at[3]))
    loads.append(pltpu.make_async_copy(mach, mc, local.at[4]))
    for c in loads:
        c.start()

    def clear(ref):
        def go(x, _):
            @pl.when(iy == 0)
            def _():
                ref[x, :, :, pl.ds(0, 8), :] = jnp.zeros(ref.shape[1:3] + (8, L), F32)
            @pl.when(iy == 1)
            def _():
                ref[x, :, :, pl.ds(24, 8), :] = jnp.zeros(ref.shape[1:3] + (8, L), F32)
            return 0
        lax.fori_loop(0, ref.shape[0], go, 0)

    def clear_x(ref, width):
        n = ref.shape[0]
        @pl.when(jnp.logical_not(has_l))
        def _():
            for x in range(width):
                ref[x, :, :, ROWS, :] = jnp.zeros(ref.shape[1:3] + (NY, L), F32)
        @pl.when(jnp.logical_not(has_r))
        def _():
            for x in range(n - width, n):
                ref[x, :, :, ROWS, :] = jnp.zeros(ref.shape[1:3] + (NY, L), F32)

    bar = pltpu.get_barrier_semaphore()

    @pl.when(has_l)
    def _():
        pl.semaphore_signal(bar, inc=1, device_id=left, device_id_type=MESH)

    @pl.when(has_r)
    def _():
        pl.semaphore_signal(bar, inc=1, device_id=right, device_id_type=MESH)

    pl.semaphore_signal(bar, inc=1, device_id=side, device_id_type=MESH)
    pl.semaphore_signal(bar, inc=1, device_id=twin, device_id_type=MESH)

    for ref, width in ((v0, 1), (v1, 1)):
        clear(ref)
        clear_x(ref, width)
    for n in range(STAGES):
        clear(f.at[n])
        clear_x(f.at[n], EX)
    for n in range(2):
        @pl.when(jnp.logical_not(has_l))
        def _():
            tb[n, 0] = jnp.zeros(tb.shape[2:], F32)
        @pl.when(jnp.logical_not(has_r))
        def _():
            tb[n, 1] = jnp.zeros(tb.shape[2:], F32)

    for c in loads:
        c.wait()

    flow = jnp.transpose(mc[...])
    for x in range(NA):
        mb[x] = jnp.broadcast_to(flow[:, x:x + 1], (NY, L))

    for m in range(-1, 5):
        for j in range(6):
            b = 2 * m - 2 + j
            if not 0 <= b < 8:
                continue
            if j in (2, 3):
                t = tl[b, 0]
            else:
                way = 1.0 if j < 2 else -1.0
                w = 0.5 + 0.5 * way * offs[b].astype(F32)
                t = (tl[b, 1].astype(F32) * w).astype(BF16)
            wk[m + 1, pl.ds(j * 128, 64), :] = t
            wk[m + 1, pl.ds(j * 128 + 64, 64), :] = t

    def relayout(x, _):
        for h in range(2):
            for c in range(4):
                f[0, x + EX, c, h, ROWS, :] = stage[pl.ds(x * 128 + h * 4 + c, NY, stride=8), :]
        return 0

    lax.fori_loop(0, NA, relayout, 0)

    pl.semaphore_wait(bar, 2 + has_l.astype(jnp.int32) + has_r.astype(jnp.int32))

    def remote(k, src, dst, to):
        return pltpu.make_async_remote_copy(src, dst, send.at[k], recv.at[k], device_id=to, device_id_type=MESH)

    class Halo:
        def __init__(self, k, ref, zref, own, width):
            n = ref.shape[0]
            first, last = width, width + own
            self.right = remote(4 * k, ref.at[pl.ds(last - width, width), :, :, ROWS, :],
                                ref.at[pl.ds(0, width), :, :, ROWS, :], right)
            self.left = remote(4 * k + 1, ref.at[pl.ds(first, width), :, :, ROWS, :],
                               ref.at[pl.ds(last, width), :, :, ROWS, :], left)
            src = jnp.where(iy == 0, R0 + NY - width, R0)
            dst = jnp.where(iy == 0, R0 - width, R0 + NY)
            self.side = remote(4 * k + 2, ref.at[pl.ds(first, own), :, :, pl.ds(src, width), :],
                               ref.at[pl.ds(first, own), :, :, pl.ds(dst, width), :], side)
            self.twin = remote(4 * k + 3, ref.at[pl.ds(first, own), :, 1 - ig, ROWS, :], zref, twin)

        def start(self):
            pl.when(has_r)(self.right.start)
            pl.when(has_l)(self.left.start)
            self.side.start()
            self.twin.start()

        def wait(self):
            self.twin.wait_recv()
            self.side.wait_recv()
            pl.when(has_l)(self.right.wait_recv)
            pl.when(has_r)(self.left.wait_recv)

        def drain(self):
            pl.when(has_r)(self.right.wait_send)
            pl.when(has_l)(self.left.wait_send)
            self.side.wait_send()
            self.twin.wait_send()

    halos = [Halo(n, f.at[n], zf.at[n], NA, EX) for n in range(STAGES)]
    eddies = [Halo(STAGES + n, (v0, v1)[n], zv.at[n], NX, 1) for n in range(2)]
    base = 4 * (STAGES + 2)
    terms = [(remote(base + 2 * n, tb.at[n, 3], tb.at[n, 0], right), remote(base + 2 * n + 1, tb.at[n, 2], tb.at[n, 1], left))
             for n in range(2)]

    eddies[0].start()
    halos[0].start()

    lane = lax.broadcasted_iota(jnp.int32, (NY, L), 1)
    keep = (lane >= 64).astype(jnp.int32) == ig

    def ahead(cur, nxt, j):
        return pltpu.roll(jnp.where(lane < j, nxt, cur), L - j, 1)

    def behind(cur, prv, j):
        return pltpu.roll(jnp.where(lane >= L - j, prv, cur), j, 1)

    def eddy(n):
        src, zsrc = (v0, v1)[n], zv.at[n]

        def go(x, _):
            b, i = x // 4, lax.rem(x, 4)
            halves = [[src[x + 1, c, h, ROWS, :] for h in range(2)] for c in range(3)]
            edge = [jnp.where(keep, zsrc[x, c], 0.0) for c in range(3)]
            for h in range(2):
                grads, laps = [], []
                for c in range(3):
                    cen = halves[c][h]
                    xp, xm = src[x + 2, c, h, ROWS, :], src[x, c, h, ROWS, :]
                    yp, ym = src[x + 1, c, h, pl.ds(R0 + 1, NY), :], src[x + 1, c, h, pl.ds(R0 - 1, NY), :]
                    nxt, prv = (halves[c][1], edge[c]) if h == 0 else (edge[c], halves[c][0])
                    zp, zm = ahead(cen, nxt, 1), behind(cen, prv, 1)
                    grads.append((0.5 * (xp - xm), 0.5 * (yp - ym), 0.5 * (zp - zm)))
                    if n == 0:
                        laps.append(((xp + xm) + (yp + ym)) + ((zp + zm) - 6.0 * cen))
                u, v, w = (halves[c][h] for c in range(3))
                ox = grads[2][1] - grads[1][2]
                oy = grads[0][2] - grads[2][0]
                oz = grads[1][0] - grads[0][1]
                lamb = (oy * w - oz * v, oz * u - ox * w, ox * v - oy * u)
                for c in range(3):
                    hi = lamb[c].astype(BF16)
                    lo = (lamb[c] - hi.astype(F32)).astype(BF16)
                    at = pl.multiple_of(b * 128 + i * 16, 16)
                    lb[pl.ds(at, 16), pl.ds((c * 2 + h) * L, L)] = hi
                    lb[pl.ds(at + 64, 16), pl.ds((c * 2 + h) * L, L)] = lo
                    if n == 0:
                        v1[x + 1, c, h, ROWS, :] = halves[c][h] + eddy_step * (viscosity * laps[c] - lamb[c])
            return 0

        lax.fori_loop(0, NX, go, 0)

    def product(m):
        j0, j1 = max(0, 2 - 2 * m), min(6, 10 - 2 * m)
        rows = pl.ds((2 * m - 2 + j0) * 128, (j1 - j0) * 128)
        return lax.dot_general(wk[m + 1, pl.ds(j0 * 128, (j1 - j0) * 128), :], lb[rows, :],
                               (((0,), (0,)), ((), ())), preferred_element_type=F32)

    def restrict(n):
        for m, slot in ((4, 3), (-1, 2)):
            r = product(m)
            for i in range(4):
                for c in range(3):
                    for h in range(2):
                        tb[n, slot, i, c, h] = r[i * 16:(i + 1) * 16, (c * 2 + h) * L:(c * 2 + h + 1) * L]
        pl.when(has_r)(terms[n][0].start)
        pl.when(has_l)(terms[n][1].start)
        for m in range(4):
            r = product(m)
            for i in range(4):
                for c in range(3):
                    for h in range(2):
                        s[n, 4 * m + i, c, h] = r[i * 16:(i + 1) * 16, (c * 2 + h) * L:(c * 2 + h + 1) * L]

    def attach(n):
        pl.when(has_l)(terms[n][0].wait_recv)
        pl.when(has_r)(terms[n][1].wait_recv)
        for i in range(4):
            s[n, i] = s[n, i] + tb[n, 0, i]
            s[n, 12 + i] = s[n, 12 + i] + tb[n, 1, i]

    def slope(ahead_, behind_):
        total = None
        for j in range(3):
            t = derivative_weights[j] * (ahead_[j] - behind_[j])
            total = t if total is None else total + t
        return total

    def rate(n, k, x):
        src, zsrc = f.at[n], zf.at[n]
        halves = [[src[x + EX, c, h, ROWS, :] for h in range(2)] for c in range(4)]
        edge = {c: jnp.where(keep, zsrc[x, c], 0.0) for c in (0, 3)}
        m = mb[x]
        result = []
        for h in range(2):
            def dx(c):
                return slope([src[x + EX + j, c, h, ROWS, :] for j in (1, 2, 3)], [src[x + EX - j, c, h, ROWS, :] for j in (1, 2, 3)])

            def dy(c):
                return slope([src[x + EX, c, h, pl.ds(R0 + j, NY), :] for j in (1, 2, 3)],
                             [src[x + EX, c, h, pl.ds(R0 - j, NY), :] for j in (1, 2, 3)])

            def dz(c):
                cen = halves[c][h]
                nxt, prv = (halves[c][1], edge[c]) if h == 0 else (edge[c], halves[c][0])
                return slope([ahead(cen, nxt, j) for j in (1, 2, 3)], [behind(cen, prv, j) for j in (1, 2, 3)])

            d = [dx(c) for c in range(4)]
            result.append((
                -(m * d[0] + d[1] + dy(2) + dz(3)),
                -(m * d[1] + d[0]) - s[k, x, 0, h],
                -(m * d[2] + dy(0)) - s[k, x, 1, h],
                -(m * d[3] + dz(0)) - s[k, x, 2, h],
            ))
        return halves, result

    def first(n, k):
        def go(x, _):
            cen, r = rate(n, k, x)
            for h in range(2):
                for c in range(4):
                    f[n + 1, x + EX, c, h, ROWS, :] = cen[c][h] + wave_step * r[h][c]
            return 0
        lax.fori_loop(0, NA, go, 0)

    def second(n, k):
        def go(x, _):
            cen, r = rate(n, k, x)
            for h in range(2):
                for c in range(4):
                    f[n + 1, x + EX, c, h, ROWS, :] = (0.5 * (f[n - 1, x + EX, c, h, ROWS, :] + cen[c][h])
                                                       + 0.5 * wave_step * r[h][c])
            return 0
        lax.fori_loop(0, NA, go, 0)

    def smooth(n, last):
        src, zsrc = f.at[n], zf.at[n]

        def go(x, _):
            for c in range(4):
                halves = [src[x + EX, c, h, ROWS, :] for h in range(2)]
                edge = jnp.where(keep, zsrc[x, c], 0.0)
                for h in range(2):
                    cen = halves[h]
                    nxt, prv = (halves[1], edge) if h == 0 else (edge, halves[0])
                    total = (1.0 - filter_weight * 3.0 * filter_taps[0]) * cen
                    for j in (1, 2, 3):
                        t = ((src[x + EX + j, c, h, ROWS, :] + src[x + EX - j, c, h, ROWS, :])
                             + (src[x + EX, c, h, pl.ds(R0 + j, NY), :] + src[x + EX, c, h, pl.ds(R0 - j, NY), :])
                             + (ahead(cen, nxt, j) + behind(cen, prv, j)))
                        total = total - (filter_weight * filter_taps[j]) * t
                    if last:
                        stage[pl.ds(x * 128 + h * 4 + c, NY, stride=8), :] = total
                    else:
                        f[n + 1, x + EX, c, h, ROWS, :] = total
            return 0
        lax.fori_loop(0, NA, go, 0)

    eddies[0].wait()
    eddy(0)
    eddies[1].start()
    restrict(0)
    eddies[1].wait()
    eddy(1)
    restrict(1)

    halos[0].wait()
    attach(0)
    first(0, 0)
    halos[1].start()
    halos[1].wait()
    second(1, 0)
    halos[2].start()
    halos[2].wait()
    smooth(2, False)
    halos[3].start()
    halos[3].wait()
    attach(1)
    first(3, 1)
    halos[4].start()
    halos[4].wait()
    second(4, 1)
    halos[5].start()
    halos[5].wait()
    smooth(5, True)
    done = pltpu.make_async_copy(stage, out, local.at[0])
    done.start()
    for h in halos + eddies:
        h.drain()
    for a, b in terms:
        pl.when(has_r)(a.wait_send)
        pl.when(has_l)(b.wait_send)
    done.wait()


def solution(mesh):
    count = mesh.shape["gx"]
    placed = (
        P("gx", "gy", None, "grp"),
        P("gx", "gy"),
        P("gx", "gy", None, None, None),
        P("gx"),
        P("gx", "gy", None, "grp"),
    )

    def body(les_velocity, mean_mach, transfer_tiles, intersection_offset, acoustic_state):
        les = les_velocity.transpose(0, 2, 1, 3)
        state = acoustic_state.reshape(NA, NY, 4, 2, L).transpose(0, 1, 3, 2, 4).reshape(NA * NY * 8, L)
        anywhere = pl.BlockSpec(memory_space=pl.ANY)
        result = pl.pallas_call(
            functools.partial(kernel, count),
            out_shape=jax.ShapeDtypeStruct(state.shape, F32),
            in_specs=[anywhere, anywhere, anywhere, pl.BlockSpec(memory_space=pltpu.SMEM), anywhere],
            out_specs=anywhere,
            scratch_shapes=[
                pltpu.VMEM((NX + 2, 3, 2, 32, L), F32),
                pltpu.VMEM((NX + 2, 3, 2, 32, L), F32),
                pltpu.VMEM((2, NX, 3, NY, L), F32),
                pltpu.VMEM((STAGES, NA + 2 * EX, 4, 2, 32, L), F32),
                pltpu.VMEM((STAGES, NA, 4, NY, L), F32),
                pltpu.VMEM((NA * NY * 8, L), F32),
                pltpu.VMEM((8 * 128, 6 * L), BF16),
                pltpu.VMEM((6, 768, 64), BF16),
                pltpu.VMEM((2, NA, 3, 2, NY, L), F32),
                pltpu.VMEM((2, 4, 4, 3, 2, NY, L), F32),
                pltpu.VMEM((NA, NY, L), F32),
                pltpu.VMEM((8, 2, 64, 64), BF16),
                pltpu.VMEM((NA, NY), F32),
                pltpu.SemaphoreType.DMA((4 * (STAGES + 2) + 4,)),
                pltpu.SemaphoreType.DMA((4 * (STAGES + 2) + 4,)),
                pltpu.SemaphoreType.DMA((8,)),
            ],
            compiler_params=pltpu.CompilerParams(collective_id=0, has_side_effects=True, vmem_limit_bytes=60 << 20),
        )(les, mean_mach, transfer_tiles[:, 0], intersection_offset, state)
        return result.reshape(NA, NY, 2, 4, L).transpose(0, 1, 3, 2, 4).reshape(acoustic_state.shape)

    return jax.shard_map(body, mesh=mesh, in_specs=placed, out_specs=P("gx", "gy", None, "grp"), check_vma=False)
```

```python
import functools

import jax
import jax.numpy as jnp
from jax import lax
from jax.experimental import pallas as pl
from jax.experimental.pallas import tpu as pltpu
from jax.sharding import PartitionSpec as P

MESH = pl.DeviceIdType.MESH
F32, BF16 = jnp.float32, jnp.bfloat16

eddy_step = 0.1
viscosity = 0.5
wave_step = 0.2
filter_weight = 0.2
derivative_weights = (0.770882380518, -0.166705904415, 0.02084314277)
filter_taps = (0.28739284246, -0.226146951809, 0.10630357877, -0.023853048191)

NX, NA, NY, L = 32, 16, 16, 128
R0 = 8
EX = 3
STAGES = 6
QV, QP, QW, QU = 0, 1, 2, 3
ORDER = (QP, QU, QV, QW)
ROWS = pl.ds(R0, NY)


def kernel(count, les, mach, tiles, offs, state, out, v0, v1, zv, f, zf, stage, lb, wk, s, tb, mb, tl, mc,
           send, recv, local):
    ix, iy, ig = lax.axis_index("gx"), lax.axis_index("gy"), lax.axis_index("grp")
    has_l, has_r = ix > 0, ix < count - 1
    right = {"gx": jnp.minimum(ix + 1, count - 1)}
    left = {"gx": jnp.maximum(ix - 1, 0)}
    side, twin = {"gy": 1 - iy}, {"grp": 1 - ig}

    bar = pltpu.get_barrier_semaphore()

    @pl.when(has_l)
    def _():
        pl.semaphore_signal(bar, inc=1, device_id=left, device_id_type=MESH)

    @pl.when(has_r)
    def _():
        pl.semaphore_signal(bar, inc=1, device_id=right, device_id_type=MESH)

    pl.semaphore_signal(bar, inc=1, device_id=side, device_id_type=MESH)
    pl.semaphore_signal(bar, inc=1, device_id=twin, device_id_type=MESH)

    loads = []
    for h in range(2):
        loads.append(pltpu.make_async_copy(les.at[:, :, :, pl.ds(L * h, L)], v0.at[pl.ds(1, NX), :, h, ROWS, :], local.at[h]))
    loads.append(pltpu.make_async_copy(state, stage, local.at[2]))
    loads.append(pltpu.make_async_copy(tiles, tl, local.at[3]))
    loads.append(pltpu.make_async_copy(mach, mc, local.at[4]))
    for c in loads:
        c.start()

    def clear(ref, width):
        n = ref.shape[0]

        def go(x, _):
            at = pl.multiple_of(jnp.where(iy == 0, 0, 24), 8)
            ref[x, :, :, pl.ds(at, 8), :] = jnp.zeros(ref.shape[1:3] + (8, L), F32)
            return 0
        lax.fori_loop(width, n - width, go, 0)

        @pl.when(jnp.logical_not(has_l))
        def _():
            for x in range(width):
                ref[x, :, :, ROWS, :] = jnp.zeros(ref.shape[1:3] + (NY, L), F32)

        @pl.when(jnp.logical_not(has_r))
        def _():
            for x in range(n - width, n):
                ref[x, :, :, ROWS, :] = jnp.zeros(ref.shape[1:3] + (NY, L), F32)

    def remote(src, dst, to):
        k = remote.count
        remote.count += 1
        return pltpu.make_async_remote_copy(src, dst, send.at[k], recv.at[k], device_id=to, device_id_type=MESH)

    remote.count = 0
    sent = []

    class Sides:
        def __init__(self, pairs):
            self.low, self.high = [remote(*pairs[0], right)], [remote(*pairs[1], left)]
            sent.append(self)

        def start(self):
            pl.when(has_r)(self.low[0].start)
            pl.when(has_l)(self.high[0].start)

        def wait(self):
            pl.when(has_l)(self.low[0].wait_recv)
            pl.when(has_r)(self.high[0].wait_recv)

        def drain(self):
            pl.when(has_r)(self.low[0].wait_send)
            pl.when(has_l)(self.high[0].wait_send)

    class Cross:
        def __init__(self, ref, zref, margin, width, x0, nx, all_fields):
            at, zat = pl.ds(margin + x0, nx), pl.ds(x0, nx)
            fy, fz = (slice(None),) * 2 if all_fields else (pl.ds(QV, 2), pl.ds(QP, 2))
            src = jnp.where(iy == 0, R0 + NY - width, R0)
            dst = jnp.where(iy == 0, R0 - width, R0 + NY)
            self.side = remote(ref.at[at, fy, :, pl.ds(src, width), :], ref.at[at, fy, :, pl.ds(dst, width), :], side)
            self.twin = remote(ref.at[at, fz, 1 - ig, ROWS, :], zref.at[zat, fz], twin)
            sent.append(self)

        def start(self):
            self.side.start()
            self.twin.start()

        def wait(self):
            self.twin.wait_recv()
            self.side.wait_recv()

        def drain(self):
            self.side.wait_send()
            self.twin.wait_send()

    def layers(ref, margin, own, width, fields, h):
        def at(x0):
            return ref.at[pl.ds(margin + x0, width), :, h, ROWS, :] if h is not None else ref.at[pl.ds(margin + x0, width), :, :, ROWS, :]
        return Sides(((at(own - width), at(-width)), (at(0), at(own))))

    veils = [(layers(v, 1, NX, 1, 3, None), Cross(v, zv.at[n], 1, 1, 0, NX, True)) for n, v in enumerate((v0, v1))]
    sides, cross = [], []
    for n in range(STAGES):
        sides.append([layers(f.at[n], EX, NA, EX, 4, h) for h in range(2)] if n else [layers(f.at[n], EX, NA, EX, 4, None)])
        cuts = (((0, NA),), ((4, 8), (0, 4), (12, 4)))[n] if n < 2 else ((3, 10), (0, 3), (13, 3))
        cross.append([Cross(f.at[n], zf.at[n], EX, EX, x0, nx, n in (2, 5)) for x0, nx in cuts])
    terms = [[Sides(((tb.at[n, 3, h], tb.at[n, 0, h]), (tb.at[n, 2, h], tb.at[n, 1, h]))) for h in range(2)] for n in range(2)]

    clear(v0, 1)
    loads[0].wait()
    loads[1].wait()
    pl.semaphore_wait(bar, 2 + has_l.astype(jnp.int32) + has_r.astype(jnp.int32))
    veils[0][0].start()
    veils[0][1].start()

    loads[2].wait()

    def relayout(x, _):
        for h in range(2):
            for c in range(4):
                f[0, x + EX, ORDER[c], h, ROWS, :] = stage[pl.ds(x * 128 + h * 4 + c, NY, stride=8), :]
        return 0

    lax.fori_loop(0, NA, relayout, 0)
    sides[0][0].start()
    cross[0][0].start()

    clear(v1, 1)
    for n in range(STAGES):
        clear(f.at[n], EX)
    for n in range(2):
        @pl.when(jnp.logical_not(has_l))
        def _():
            tb[n, 0] = jnp.zeros(tb.shape[2:], F32)

        @pl.when(jnp.logical_not(has_r))
        def _():
            tb[n, 1] = jnp.zeros(tb.shape[2:], F32)

    loads[3].wait()
    loads[4].wait()

    flow = jnp.transpose(mc[...])
    for x in range(NA):
        mb[x] = jnp.broadcast_to(flow[:, x:x + 1], (NY, L))

    for m in range(-1, 5):
        for j in range(6):
            b = 2 * m - 2 + j
            if not 0 <= b < 8:
                continue
            if j in (2, 3):
                t = tl[b, 0]
            else:
                way = 1.0 if j < 2 else -1.0
                w = 0.5 + 0.5 * way * offs[b].astype(F32)
                t = (tl[b, 1].astype(F32) * w).astype(BF16)
            wk[m + 1, pl.ds(j * 128, 64), :] = t
            wk[m + 1, pl.ds(j * 128 + 64, 64), :] = t

    lane = lax.broadcasted_iota(jnp.int32, (NY, L), 1)
    keep = (lane >= 64).astype(jnp.int32) == ig

    def ahead(cur, nxt, j):
        return pltpu.roll(jnp.where(lane < j, nxt, cur), L - j, 1)

    def behind(cur, prv, j):
        return pltpu.roll(jnp.where(lane >= L - j, prv, cur), j, 1)

    def eddy(n, x):
        src, zsrc = (v0, v1)[n], zv.at[n]
        b, i = x // 4, lax.rem(x, 4)
        halves = [[src[x + 1, c, h, ROWS, :] for h in range(2)] for c in range(3)]
        edge = [jnp.where(keep, zsrc[x, c], 0.0) for c in range(3)]
        for h in range(2):
            grads, laps = [], []
            for c in range(3):
                cen = halves[c][h]
                xp, xm = src[x + 2, c, h, ROWS, :], src[x, c, h, ROWS, :]
                yp, ym = src[x + 1, c, h, pl.ds(R0 + 1, NY), :], src[x + 1, c, h, pl.ds(R0 - 1, NY), :]
                if n == 0 or c < 2:
                    nxt, prv = (halves[c][1], edge[c]) if h == 0 else (edge[c], halves[c][0])
                    zp, zm = ahead(cen, nxt, 1), behind(cen, prv, 1)
                else:
                    zp = zm = cen
                grads.append((0.5 * (xp - xm), 0.5 * (yp - ym), 0.5 * (zp - zm)))
                if n == 0:
                    laps.append(((xp + xm) + (yp + ym)) + ((zp + zm) - 6.0 * cen))
            u, v, w = (halves[c][h] for c in range(3))
            ox = grads[2][1] - grads[1][2]
            oy = grads[0][2] - grads[2][0]
            oz = grads[1][0] - grads[0][1]
            lamb = (oy * w - oz * v, oz * u - ox * w, ox * v - oy * u)
            for c in range(3):
                hi = lamb[c].astype(BF16)
                lo = (lamb[c] - hi.astype(F32)).astype(BF16)
                at = pl.multiple_of(b * 128 + i * 16, 16)
                lb[pl.ds(at, 16), pl.ds((h * 3 + c) * L, L)] = hi
                lb[pl.ds(at + 64, 16), pl.ds((h * 3 + c) * L, L)] = lo
                if n == 0:
                    v1[x + 1, c, h, ROWS, :] = halves[c][h] + eddy_step * (viscosity * laps[c] - lamb[c])

    def product(m, h=None):
        j0, j1 = max(0, 2 - 2 * m), min(6, 10 - 2 * m)
        rows = pl.ds((2 * m - 2 + j0) * 128, (j1 - j0) * 128)
        cols = pl.ds(0, 6 * L) if h is None else pl.ds(h * 3 * L, 3 * L)
        return lax.dot_general(wk[m + 1, pl.ds(j0 * 128, (j1 - j0) * 128), :], lb[rows, cols],
                               (((0,), (0,)), ((), ())), preferred_element_type=F32)

    def rim_terms(n, h):
        for m, slot in ((4, 3), (-1, 2)):
            r = product(m, h)
            for i in range(4):
                for c in range(3):
                    tb[n, slot, h, i, c] = r[i * 16:(i + 1) * 16, c * L:(c + 1) * L]

    def own_terms(n):
        for m in range(4):
            r = product(m)
            for i in range(4):
                for c in range(3):
                    for h in range(2):
                        s[n, 4 * m + i, c, h] = r[i * 16:(i + 1) * 16, (h * 3 + c) * L:(h * 3 + c + 1) * L]

    def attach(n, h):
        for i in range(4):
            for c in range(3):
                s[n, i, c, h] = s[n, i, c, h] + tb[n, 0, h, i, c]
                s[n, 12 + i, c, h] = s[n, 12 + i, c, h] + tb[n, 1, h, i, c]

    def slope(ahead_, behind_):
        total = None
        for j in range(3):
            t = derivative_weights[j] * (ahead_[j] - behind_[j])
            total = t if total is None else total + t
        return total

    def beside(n, x, c, h):
        edge = jnp.where(keep, zf[n, x, c], 0.0)
        other = f[n, x + EX, c, 1 - h, ROWS, :]
        return (other, edge) if h == 0 else (edge, other)

    def rate(n, k, x, h):
        src = f.at[n]
        cen = [src[x + EX, c, h, ROWS, :] for c in range(4)]
        m = mb[x]

        def dx(c):
            return slope([src[x + EX + j, c, h, ROWS, :] for j in (1, 2, 3)], [src[x + EX - j, c, h, ROWS, :] for j in (1, 2, 3)])

        def dy(c):
            return slope([src[x + EX, c, h, pl.ds(R0 + j, NY), :] for j in (1, 2, 3)],
                         [src[x + EX, c, h, pl.ds(R0 - j, NY), :] for j in (1, 2, 3)])

        def dz(c):
            nxt, prv = beside(n, x, c, h)
            return slope([ahead(cen[c], nxt, j) for j in (1, 2, 3)], [behind(cen[c], prv, j) for j in (1, 2, 3)])

        d = [dx(c) for c in range(4)]
        r = [None] * 4
        r[QP] = -(m * d[QP] + d[QU] + dy(QV) + dz(QW))
        r[QU] = -(m * d[QU] + d[QP]) - s[k, x, 0, h]
        r[QV] = -(m * d[QV] + dy(QP)) - s[k, x, 1, h]
        r[QW] = -(m * d[QW] + dz(QP)) - s[k, x, 2, h]
        return cen, r

    def first(n, k, x, h):
        cen, r = rate(n, k, x, h)
        for c in range(4):
            f[n + 1, x + EX, c, h, ROWS, :] = cen[c] + wave_step * r[c]

    def second(n, k, x, h):
        cen, r = rate(n, k, x, h)
        for c in range(4):
            f[n + 1, x + EX, c, h, ROWS, :] = 0.5 * (f[n - 1, x + EX, c, h, ROWS, :] + cen[c]) + 0.5 * wave_step * r[c]

    def smooth(n, x, h):
        src = f.at[n]
        for q, c in enumerate(ORDER):
            cen = src[x + EX, c, h, ROWS, :]
            nxt, prv = beside(n, x, c, h)
            total = (1.0 - filter_weight * 3.0 * filter_taps[0]) * cen
            for j in (1, 2, 3):
                t = ((src[x + EX + j, c, h, ROWS, :] + src[x + EX - j, c, h, ROWS, :])
                     + (src[x + EX, c, h, pl.ds(R0 + j, NY), :] + src[x + EX, c, h, pl.ds(R0 - j, NY), :])
                     + (ahead(cen, nxt, j) + behind(cen, prv, j)))
                total = total - (filter_weight * filter_taps[j]) * t
            if n + 1 == STAGES:
                stage[pl.ds(x * 128 + h * 4 + q, NY, stride=8), :] = total
            else:
                f[n + 1, x + EX, c, h, ROWS, :] = total

    def over(lo, hi, step):
        def go(x, _):
            step(x)
            return 0
        lax.fori_loop(lo, hi, go, 0)

    def both(step):
        def go(x):
            step(x, 0)
            step(x, 1)
        return go

    def rim(width, step):
        def go(i):
            step(jnp.where(i < width, i, i + NA - 2 * width))
        over(0, 2 * width, go)

    veils[0][1].wait()
    over(1, NX - 1, functools.partial(eddy, 0))
    veils[0][0].wait()
    over(0, 2, lambda i: eddy(0, i * (NX - 1)))
    for h in range(2):
        rim_terms(0, h)
        terms[0][h].start()
    for c in veils[1]:
        c.start()
    own_terms(0)

    cross[0][0].wait()
    sides[0][0].wait()
    over(0, NA, both(functools.partial(first, 0, 0)))
    cross[1][0].start()
    for h in range(2):
        terms[0][h].wait()

        def mend(i):
            for c, q in enumerate((QU, QV, QW)):
                for x0, slot in ((0, 0), (12, 1)):
                    old = f[1, x0 + i + EX, q, h, ROWS, :]
                    f[1, x0 + i + EX, q, h, ROWS, :] = old - wave_step * tb[0, slot, h, i, c]
        over(0, 4, mend)
        sides[1][h].start()
    cross[1][1].start()
    cross[1][2].start()
    for h in range(2):
        attach(0, h)

    for n in range(1, STAGES):
        step = (functools.partial(first, n, n // 3), functools.partial(second, n, n // 3), functools.partial(smooth, n))[n % 3]
        cross[n][0].wait()
        if n == 1:
            cross[n][1].wait()
            cross[n][2].wait()
        over(3, 13, both(step))
        if n + 1 < STAGES:
            cross[n + 1][0].start()
        else:
            inner = pltpu.make_async_copy(stage.at[pl.ds(3 * 128, 10 * 128)], out.at[pl.ds(3 * 128, 10 * 128)], local.at[0])
            inner.start()
        if n == 1:
            for c in veils[1]:
                c.wait()
            over(0, NX, functools.partial(eddy, 1))
            for h in range(2):
                rim_terms(1, h)
            own_terms(1)
        if n == 2:
            for h in range(2):
                terms[1][h].wait()
                attach(1, h)
        if n > 1:
            cross[n][1].wait()
            cross[n][2].wait()
        for h in range(2):
            sides[n][h].wait()
            rim(EX, lambda x: step(x, h))
            if n + 1 < STAGES:
                sides[n + 1][h].start()
        if n + 1 < STAGES:
            cross[n + 1][1].start()
            cross[n + 1][2].start()
        if n == 1:
            for h in range(2):
                terms[1][h].start()
    outer = [pltpu.make_async_copy(stage.at[pl.ds(x * 128, 3 * 128)], out.at[pl.ds(x * 128, 3 * 128)], local.at[k])
             for k, x in ((1, 0), (2, 13))]
    for c in outer:
        c.start()
    for c in sent:
        c.drain()
    inner.wait()
    for c in outer:
        c.wait()


def solution(mesh):
    count = mesh.shape["gx"]
    placed = (
        P("gx", "gy", None, "grp"),
        P("gx", "gy"),
        P("gx", "gy", None, None, None),
        P("gx"),
        P("gx", "gy", None, "grp"),
    )

    def body(les_velocity, mean_mach, transfer_tiles, intersection_offset, acoustic_state):
        les = les_velocity.transpose(0, 2, 1, 3)
        state = acoustic_state.reshape(NA, NY, 4, 2, L).transpose(0, 1, 3, 2, 4).reshape(NA * NY * 8, L)
        anywhere = pl.BlockSpec(memory_space=pl.ANY)
        result = pl.pallas_call(
            functools.partial(kernel, count),
            out_shape=jax.ShapeDtypeStruct(state.shape, F32),
            in_specs=[anywhere, anywhere, anywhere, pl.BlockSpec(memory_space=pltpu.SMEM), anywhere],
            out_specs=anywhere,
            scratch_shapes=[
                pltpu.VMEM((NX + 2, 3, 2, 32, L), F32),
                pltpu.VMEM((NX + 2, 3, 2, 32, L), F32),
                pltpu.VMEM((2, NX, 3, NY, L), F32),
                pltpu.VMEM((STAGES, NA + 2 * EX, 4, 2, 32, L), F32),
                pltpu.VMEM((STAGES, NA, 4, NY, L), F32),
                pltpu.VMEM((NA * NY * 8, L), F32),
                pltpu.VMEM((8 * 128, 6 * L), BF16),
                pltpu.VMEM((6, 768, 64), BF16),
                pltpu.VMEM((2, NA, 3, 2, NY, L), F32),
                pltpu.VMEM((2, 4, 2, 4, 3, NY, L), F32),
                pltpu.VMEM((NA, NY, L), F32),
                pltpu.VMEM((8, 2, 64, 64), BF16),
                pltpu.VMEM((NA, NY), F32),
                pltpu.SemaphoreType.DMA((72,)),
                pltpu.SemaphoreType.DMA((72,)),
                pltpu.SemaphoreType.DMA((8,)),
            ],
            compiler_params=pltpu.CompilerParams(collective_id=0, has_side_effects=True, vmem_limit_bytes=60 << 20),
        )(les, mean_mach, transfer_tiles[:, 0], intersection_offset, state)
        return result.reshape(NA, NY, 2, 4, L).transpose(0, 1, 3, 2, 4).reshape(acoustic_state.shape)

    return jax.shard_map(body, mesh=mesh, in_specs=placed, out_specs=P("gx", "gy", None, "grp"), check_vma=False)
```

```python
import functools

import jax
import jax.numpy as jnp
from jax import lax
from jax.experimental import pallas as pl
from jax.experimental.pallas import tpu as pltpu
from jax.sharding import PartitionSpec as P

MESH = pl.DeviceIdType.MESH
F32, BF16 = jnp.float32, jnp.bfloat16

eddy_step = 0.1
viscosity = 0.5
wave_step = 0.2
filter_weight = 0.2
derivative_weights = (0.770882380518, -0.166705904415, 0.02084314277)
filter_taps = (0.28739284246, -0.226146951809, 0.10630357877, -0.023853048191)

NX, NA, NY, L = 32, 16, 16, 128
R0 = 8
EX = 3
STAGES = 6
QV, QP, QW, QU = 0, 1, 2, 3
ORDER = (QP, QU, QV, QW)
ROWS = pl.ds(R0, NY)


def kernel(count, les, mach, tiles, offs, state, out, *refs):
    (v0, v1, *zv), refs = refs[:4], refs[4:]
    f, zf, xh, yh, refs = *(refs[k * STAGES:(k + 1) * STAGES] for k in range(4)), refs[4 * STAGES:]
    s, tb, (stage, lb, wk, mb, tl, mc, send, recv, local) = refs[:2], refs[2:4], refs[4:]
    ix, iy, ig = lax.axis_index("gx"), lax.axis_index("gy"), lax.axis_index("grp")
    has_l, has_r = ix > 0, ix < count - 1
    right = {"gx": jnp.minimum(ix + 1, count - 1)}
    left = {"gx": jnp.maximum(ix - 1, 0)}
    side, twin = {"gy": 1 - iy}, {"grp": 1 - ig}
    later = ((ix == count // 2 - 1) | (ix == count // 2)) & (iy == 1)
    sooner = jnp.logical_not(later)

    bar = pltpu.get_barrier_semaphore()

    @pl.when(has_l)
    def _():
        pl.semaphore_signal(bar, inc=1, device_id=left, device_id_type=MESH)

    @pl.when(has_r)
    def _():
        pl.semaphore_signal(bar, inc=1, device_id=right, device_id_type=MESH)

    pl.semaphore_signal(bar, inc=1, device_id=side, device_id_type=MESH)
    pl.semaphore_signal(bar, inc=1, device_id=twin, device_id_type=MESH)

    loads = []
    for h in range(2):
        loads.append(pltpu.make_async_copy(les.at[:, :, :, pl.ds(L * h, L)], v0.at[pl.ds(1, NX), :, h, ROWS, :], local.at[h]))
    loads.append(pltpu.make_async_copy(state, stage, local.at[2]))
    loads.append(pltpu.make_async_copy(tiles, tl, local.at[3]))
    loads.append(pltpu.make_async_copy(mach, mc, local.at[4]))
    for c in loads:
        c.start()

    def clear(ref, width, always):
        n = ref.shape[0]

        def go(x, _):
            if always:
                for at in (0, 24):
                    ref[x, :, :, pl.ds(at, 8), :] = jnp.zeros(ref.shape[1:3] + (8, L), F32)
            else:
                at = pl.multiple_of(jnp.where(iy == 0, 0, 24), 8)
                ref[x, :, :, pl.ds(at, 8), :] = jnp.zeros(ref.shape[1:3] + (8, L), F32)
            return 0
        lax.fori_loop(width, n - width, go, 0)

        def ends(low):
            for x in range(width):
                ref[x if low else n - 1 - x, :, :, ROWS, :] = jnp.zeros(ref.shape[1:3] + (NY, L), F32)

        if always:
            ends(True)
            ends(False)
        else:
            pl.when(jnp.logical_not(has_l))(lambda: ends(True))
            pl.when(jnp.logical_not(has_r))(lambda: ends(False))

    def clear_rows(ref):
        def go(x, _):
            at = pl.multiple_of(8 * iy, 8)
            ref[x, :, :, pl.ds(at, 8), :] = jnp.zeros(ref.shape[1:3] + (8, L), F32)
            return 0
        lax.fori_loop(0, NA, go, 0)

    def remote(src, dst, to):
        k = remote.count
        remote.count += 1
        return pltpu.make_async_remote_copy(src, dst, send.at[k], recv.at[k], device_id=to, device_id_type=MESH)

    remote.count = 0
    sent = []

    class Sides:
        def __init__(self, pairs):
            self.low, self.high = [remote(*pairs[0], right)], [remote(*pairs[1], left)]
            sent.append(self)

        def start(self):
            pl.when(has_r)(self.low[0].start)
            pl.when(has_l)(self.high[0].start)

        def wait(self):
            pl.when(has_l)(self.low[0].wait_recv)
            pl.when(has_r)(self.high[0].wait_recv)

        def drain(self):
            pl.when(has_r)(self.low[0].wait_send)
            pl.when(has_l)(self.high[0].wait_send)

    class Cross:
        def __init__(self, ref, yref, zref, margin, width, x0, nx, all_fields):
            at, zat = pl.ds(margin + x0, nx), pl.ds(x0, nx)
            fy, fz = (slice(None),) * 2 if all_fields else (pl.ds(QV, 2), pl.ds(QP, 2))
            src = jnp.where(iy == 0, R0 + NY - width, R0)
            dst = jnp.where(iy == 0, R0 - width, R0 + NY)
            self.heard = False
            if yref is None:
                target = ref.at[at, fy, :, pl.ds(dst, width), :]
            else:
                target = yref.at[zat, fy, :, pl.ds(jnp.where(iy == 0, 8 - width, 8), width), :]
            self.side = remote(ref.at[at, fy, :, pl.ds(src, width), :], target, side)
            self.twin = remote(ref.at[at, fz, 1 - ig, ROWS, :], zref.at[zat, fz], twin)
            sent.append(self)

        def start(self):
            self.side.start()
            self.twin.start()

        def wait(self):
            self.wait_twin()
            self.wait_side()

        def wait_twin(self):
            self.twin.wait_recv()

        def wait_side(self):
            if self.heard:
                pl.when(sooner)(self.side.wait_recv)
            else:
                self.side.wait_recv()

        def hear(self):
            self.heard = True
            self.side.wait_recv()

        def drain(self):
            self.side.wait_send()
            self.twin.wait_send()

    def rims(n, h):
        half = slice(None) if h is None else h
        return Sides(((f[n].at[pl.ds(EX + NA - EX, EX), :, half, ROWS, :], xh[n].at[0, :, :, half]),
                      (f[n].at[pl.ds(EX, EX), :, half, ROWS, :], xh[n].at[1, :, :, half])))

    def veil(v):
        return Sides(((v.at[pl.ds(NX, 1), :, :, ROWS, :], v.at[pl.ds(0, 1), :, :, ROWS, :]),
                      (v.at[pl.ds(1, 1), :, :, ROWS, :], v.at[pl.ds(NX + 1, 1), :, :, ROWS, :])))

    veils = [(veil(v), Cross(v, None, zv[n], 1, 1, 0, NX, True)) for n, v in enumerate((v0, v1))]
    sides, cross = [], []
    for n in range(STAGES):
        sides.append([rims(n, h) for h in range(2)])
        cuts = ((0, NA),) if n == 0 else ((4, 8), (0, 4), (12, 4)) if n % 3 == 1 else ((3, 10), (0, 3), (13, 3))
        cross.append([Cross(f[n], yh[n], zf[n], EX, EX, x0, nx, n in (2, 5)) for x0, nx in cuts])
    terms = [[Sides(((tb[n].at[3, h], tb[n].at[0, h]), (tb[n].at[2, h], tb[n].at[1, h]))) for h in range(2)] for n in range(2)]

    clear(v0, 1, False)
    loads[0].wait()
    loads[1].wait()
    pl.semaphore_wait(bar, 2 + has_l.astype(jnp.int32) + has_r.astype(jnp.int32))
    veils[0][0].start()
    veils[0][1].start()

    loads[2].wait()

    def relayout(x, _):
        for h in range(2):
            for c in range(4):
                f[0][x + EX, ORDER[c], h, ROWS, :] = stage[pl.ds(x * 128 + h * 4 + c, NY, stride=8), :]
        return 0

    lax.fori_loop(0, NA, relayout, 0)
    for h in range(2):
        sides[0][h].start()
    cross[0][0].start()
    clear(f[0], EX, True)
    clear_rows(yh[0])

    clear(v1, 1, False)
    for n in range(1, STAGES):
        clear(f[n], EX, True)
        clear_rows(yh[n])
    for n in range(2):
        @pl.when(jnp.logical_not(has_l))
        def _():
            tb[n][0] = jnp.zeros(tb[n].shape[1:], F32)

        @pl.when(jnp.logical_not(has_r))
        def _():
            tb[n][1] = jnp.zeros(tb[n].shape[1:], F32)

    loads[3].wait()
    loads[4].wait()

    flow = jnp.transpose(mc[...])
    for x in range(NA):
        mb[x] = jnp.broadcast_to(flow[:, x:x + 1], (NY, L))

    for m in range(-1, 5):
        for j in range(6):
            b = 2 * m - 2 + j
            if not 0 <= b < 8:
                continue
            if j in (2, 3):
                t = tl[b, 0]
            else:
                way = 1.0 if j < 2 else -1.0
                w = 0.5 + 0.5 * way * offs[b].astype(F32)
                t = (tl[b, 1].astype(F32) * w).astype(BF16)
            wk[m + 1, pl.ds(j * 128, 64), :] = t
            wk[m + 1, pl.ds(j * 128 + 64, 64), :] = t

    lane = lax.broadcasted_iota(jnp.int32, (NY, L), 1)
    keep = (lane >= 64).astype(jnp.int32) == ig

    def ahead(cur, nxt, j):
        return pltpu.roll(jnp.where(lane < j, nxt, cur), L - j, 1)

    def behind(cur, prv, j):
        return pltpu.roll(jnp.where(lane >= L - j, prv, cur), j, 1)

    def eddy(n, x):
        src, zsrc = (v0, v1)[n], zv[n]
        b, i = x // 4, lax.rem(x, 4)
        halves = [[src[x + 1, c, h, ROWS, :] for h in range(2)] for c in range(3)]
        edge = [jnp.where(keep, zsrc[x, c], 0.0) for c in range(3)]
        for h in range(2):
            grads, laps = [], []
            for c in range(3):
                cen = halves[c][h]
                xp, xm = src[x + 2, c, h, ROWS, :], src[x, c, h, ROWS, :]
                yp, ym = src[x + 1, c, h, pl.ds(R0 + 1, NY), :], src[x + 1, c, h, pl.ds(R0 - 1, NY), :]
                if n == 0 or c < 2:
                    nxt, prv = (halves[c][1], edge[c]) if h == 0 else (edge[c], halves[c][0])
                    zp, zm = ahead(cen, nxt, 1), behind(cen, prv, 1)
                else:
                    zp = zm = cen
                grads.append((0.5 * (xp - xm), 0.5 * (yp - ym), 0.5 * (zp - zm)))
                if n == 0:
                    laps.append(((xp + xm) + (yp + ym)) + ((zp + zm) - 6.0 * cen))
            u, v, w = (halves[c][h] for c in range(3))
            ox = grads[2][1] - grads[1][2]
            oy = grads[0][2] - grads[2][0]
            oz = grads[1][0] - grads[0][1]
            lamb = (oy * w - oz * v, oz * u - ox * w, ox * v - oy * u)
            for c in range(3):
                hi = lamb[c].astype(BF16)
                lo = (lamb[c] - hi.astype(F32)).astype(BF16)
                at = pl.multiple_of(b * 128 + i * 16, 16)
                lb[pl.ds(at, 16), pl.ds((h * 3 + c) * L, L)] = hi
                lb[pl.ds(at + 64, 16), pl.ds((h * 3 + c) * L, L)] = lo
                if n == 0:
                    v1[x + 1, c, h, ROWS, :] = halves[c][h] + eddy_step * (viscosity * laps[c] - lamb[c])

    def product(m, h=None):
        j0, j1 = max(0, 2 - 2 * m), min(6, 10 - 2 * m)
        rows = pl.ds((2 * m - 2 + j0) * 128, (j1 - j0) * 128)
        cols = pl.ds(0, 6 * L) if h is None else pl.ds(h * 3 * L, 3 * L)
        return lax.dot_general(wk[m + 1, pl.ds(j0 * 128, (j1 - j0) * 128), :], lb[rows, cols],
                               (((0,), (0,)), ((), ())), preferred_element_type=F32)

    def rim_terms(n, h):
        for m, slot in ((4, 3), (-1, 2)):
            r = product(m, h)
            for i in range(4):
                for c in range(3):
                    tb[n][slot, h, i, c] = r[i * 16:(i + 1) * 16, c * L:(c + 1) * L]

    def own_terms(n):
        for m in range(4):
            r = product(m)
            for i in range(4):
                for c in range(3):
                    for h in range(2):
                        s[n][4 * m + i, c, h] = r[i * 16:(i + 1) * 16, (h * 3 + c) * L:(h * 3 + c + 1) * L]

    def attach(n, h):
        for i in range(4):
            for c in range(3):
                s[n][i, c, h] = s[n][i, c, h] + tb[n][0, h, i, c]
                s[n][12 + i, c, h] = s[n][12 + i, c, h] + tb[n][1, h, i, c]

    def slope(ahead_, behind_):
        total = None
        for j in range(3):
            t = derivative_weights[j] * (ahead_[j] - behind_[j])
            total = t if total is None else total + t
        return total

    def beside(n, x, c, h):
        edge = jnp.where(keep, zf[n][x, c], 0.0)
        other = f[n][x + EX, c, 1 - h, ROWS, :]
        return (other, edge) if h == 0 else (edge, other)

    def rate(n, k, x, h):
        src = f[n]
        cen = [src[x + EX, c, h, ROWS, :] for c in range(4)]
        m = mb[x]

        def dx(c):
            return slope([src[x + EX + j, c, h, ROWS, :] for j in (1, 2, 3)], [src[x + EX - j, c, h, ROWS, :] for j in (1, 2, 3)])

        def dy(c):
            return slope([src[x + EX, c, h, pl.ds(R0 + j, NY), :] for j in (1, 2, 3)],
                         [src[x + EX, c, h, pl.ds(R0 - j, NY), :] for j in (1, 2, 3)])

        def dz(c):
            nxt, prv = beside(n, x, c, h)
            return slope([ahead(cen[c], nxt, j) for j in (1, 2, 3)], [behind(cen[c], prv, j) for j in (1, 2, 3)])

        d = [dx(c) for c in range(4)]
        r = [None] * 4
        r[QP] = -(m * d[QP] + d[QU] + dy(QV) + dz(QW))
        r[QU] = -(m * d[QU] + d[QP]) - s[k][x, 0, h]
        r[QV] = -(m * d[QV] + dy(QP)) - s[k][x, 1, h]
        r[QW] = -(m * d[QW] + dz(QP)) - s[k][x, 2, h]
        return cen, r

    def first(n, k, x, h):
        cen, r = rate(n, k, x, h)
        for c in range(4):
            f[n + 1][x + EX, c, h, ROWS, :] = cen[c] + wave_step * r[c]

    def second(n, k, x, h):
        cen, r = rate(n, k, x, h)
        for c in range(4):
            f[n + 1][x + EX, c, h, ROWS, :] = 0.5 * (f[n - 1][x + EX, c, h, ROWS, :] + cen[c]) + 0.5 * wave_step * r[c]

    def smooth(n, x, h):
        src = f[n]
        for q, c in enumerate(ORDER):
            cen = src[x + EX, c, h, ROWS, :]
            nxt, prv = beside(n, x, c, h)
            total = (1.0 - filter_weight * 3.0 * filter_taps[0]) * cen
            for j in (1, 2, 3):
                t = ((src[x + EX + j, c, h, ROWS, :] + src[x + EX - j, c, h, ROWS, :])
                     + (src[x + EX, c, h, pl.ds(R0 + j, NY), :] + src[x + EX, c, h, pl.ds(R0 - j, NY), :])
                     + (ahead(cen, nxt, j) + behind(cen, prv, j)))
                total = total - (filter_weight * filter_taps[j]) * t
            if n + 1 == STAGES:
                stage[pl.ds(x * 128 + h * 4 + q, NY, stride=8), :] = total
            else:
                f[n + 1][x + EX, c, h, ROWS, :] = total

    def correct_rows(n, x):
        kind = n % 3
        taps = [filter_weight * w for w in filter_taps[1:]] if kind == 2 else derivative_weights
        w = wave_step if kind == 0 else 0.5 * wave_step

        def side_of(low):
            own = 0 if low else 8
            for h in range(2):
                for c in range(4) if kind == 2 else (QV, QP):
                    total = None
                    for j in (1, 2, 3):
                        p = taps[j - 1] * yh[n][x, c, h, pl.ds(8 - j if low else j, 8), :]
                        total = p if total is None else total + p
                    to = c if kind == 2 else QP + QV - c
                    if n + 1 == STAGES:
                        at = pl.ds(x * 128 + own * 8 + h * 4 + ORDER.index(c), 8, stride=8)
                        stage[at, :] = stage[at, :] - total
                    else:
                        at = pl.ds(R0 + own, 8)
                        change = total if kind == 2 else (-w if low else w) * total
                        f[n + 1][x + EX, to, h, at, :] = f[n + 1][x + EX, to, h, at, :] - change

        pl.when(iy == 1)(lambda: side_of(True))
        pl.when(iy == 0)(lambda: side_of(False))

    def correct(n, h):
        kind = n % 3
        taps = [filter_weight * w for w in filter_taps[1:]] if kind == 2 else derivative_weights

        def side_of(low):
            halo = [[xh[n][0 if low else 1, EX - k if low else k - 1, c, h] for c in range(4)] for k in (1, 2, 3)]
            for i in range(EX):
                x = i if low else NA - 1 - i
                d = []
                for c in range(4):
                    total = taps[i] * halo[0][c]
                    for k in range(1, EX - i):
                        total = total + taps[i + k] * halo[k][c]
                    d.append(total)
                if kind == 2:
                    change = d
                else:
                    w = (wave_step if kind == 0 else 0.5 * wave_step) * (-1.0 if low else 1.0)
                    m = w * mb[x]
                    change = [None] * 4
                    change[QP] = m * d[QP] + w * d[QU]
                    change[QU] = m * d[QU] + w * d[QP]
                    change[QV] = m * d[QV]
                    change[QW] = m * d[QW]
                for q, c in enumerate(ORDER):
                    if n + 1 == STAGES:
                        at = pl.ds(x * 128 + h * 4 + q, NY, stride=8)
                        stage[at, :] = stage[at, :] - change[c]
                    else:
                        f[n + 1][x + EX, c, h, ROWS, :] = f[n + 1][x + EX, c, h, ROWS, :] - change[c]

        pl.when(has_l)(lambda: side_of(True))
        pl.when(has_r)(lambda: side_of(False))

    def over(lo, hi, step):
        def go(x, _):
            step(lo + 2 * x)
            step(lo + 2 * x + 1)
            return 0
        lax.fori_loop(0, (hi - lo) // 2, go, 0)

    def both(step):
        def go(x):
            step(x, 0)
            step(x, 1)
        return go

    def rim(width, step):
        def go(i):
            step(jnp.where(i < width, i, i + NA - 2 * width))
        over(0, 2 * width, go)

    def mend(k):
        n = 3 * k + 1
        for h in range(2):
            sides[n][h].drain()
            sent.remove(sides[n][h])
            terms[k][h].wait()

            def go(i):
                for c, q in enumerate((QU, QV, QW)):
                    for x0, slot in ((0, 0), (12, 1)):
                        f[n][x0 + i + EX, q, h, ROWS, :] = f[n][x0 + i + EX, q, h, ROWS, :] - wave_step * tb[k][slot, h, i, c]
            over(0, 4, go)
        cross[n][1].start()
        cross[n][2].start()
        for h in range(2):
            attach(k, h)

    def mend_halo(k, h):
        n = 3 * k + 1
        for low, slot, first_layer in ((0, 2, 1), (1, 3, 0)):
            def go():
                for j in range(EX):
                    for c, q in enumerate((QU, QV, QW)):
                        xh[n][low, j, q, h] = xh[n][low, j, q, h] - wave_step * tb[k][slot, h, j + first_layer, c]
            pl.when(has_r if low else has_l)(go)

    veils[0][1].wait()
    over(1, NX - 1, functools.partial(eddy, 0))
    veils[0][0].wait()
    over(0, 2, lambda i: eddy(0, i * (NX - 1)))
    for h in range(2):
        rim_terms(0, h)
        terms[0][h].start()
    own_terms(0)

    for n in range(STAGES):
        step = (functools.partial(first, n, n // 3), functools.partial(second, n, n // 3), functools.partial(smooth, n))[n % 3]
        if n == 2:
            for c in veils[1]:
                c.wait()
            over(0, NX, functools.partial(eddy, 1))
            rim_terms(1, 0)
            terms[1][0].start()
            rim_terms(1, 1)
            own_terms(1)
        cross[n][0].wait_twin()
        if n == 0:
            over(0, NA, both(step))
        else:
            width = 4 if n % 3 == 1 else EX
            over(width, NA - width, both(step))
            cross[n][1].wait_twin()
            cross[n][2].wait_twin()
            rim(width, lambda x: both(step)(x))
        for c in cross[n]:
            c.wait_side()
        over(0, NA, functools.partial(correct_rows, n))
        if n + 1 == STAGES:
            inner = pltpu.make_async_copy(stage.at[pl.ds(3 * 128, 10 * 128)], out.at[pl.ds(3 * 128, 10 * 128)], local.at[0])
            inner.start()
        elif n % 3:
            cross[n + 1][0].start()
        for h in range(2):
            sides[n][h].wait()
            if n % 3 == 1:
                mend_halo(n // 3, h)
            correct(n, h)
            if n + 1 < STAGES:
                pl.when(sooner)(sides[n + 1][h].start)
        if n % 3 == 0:
            cross[n + 1][0].start()
        elif n + 1 < STAGES:
            cross[n + 1][1].start()
            cross[n + 1][2].start()
        if n + 1 < STAGES:
            @pl.when(later)
            def _():
                cross[n + 1][0 if n % 3 == 0 else 2].hear()
                for h in range(2):
                    sides[n + 1][h].start()
        if n % 3 == 0:
            mend(n // 3)
        if n == 0:
            for c in veils[1]:
                c.start()
        if n == 2:
            terms[1][1].start()
    outer = [pltpu.make_async_copy(stage.at[pl.ds(x * 128, 3 * 128)], out.at[pl.ds(x * 128, 3 * 128)], local.at[k])
             for k, x in ((1, 0), (2, 13))]
    for c in outer:
        c.start()
    for c in sent:
        c.drain()
    inner.wait()
    for c in outer:
        c.wait()


def solution(mesh):
    count = mesh.shape["gx"]
    placed = (
        P("gx", "gy", None, "grp"),
        P("gx", "gy"),
        P("gx", "gy", None, None, None),
        P("gx"),
        P("gx", "gy", None, "grp"),
    )

    def body(les_velocity, mean_mach, transfer_tiles, intersection_offset, acoustic_state):
        les = les_velocity.transpose(0, 2, 1, 3)
        state = acoustic_state.reshape(NA, NY, 4, 2, L).transpose(0, 1, 3, 2, 4).reshape(NA * NY * 8, L)
        anywhere = pl.BlockSpec(memory_space=pl.ANY)
        result = pl.pallas_call(
            functools.partial(kernel, count),
            out_shape=jax.ShapeDtypeStruct(state.shape, F32),
            in_specs=[anywhere, anywhere, anywhere, pl.BlockSpec(memory_space=pltpu.SMEM), anywhere],
            out_specs=anywhere,
            scratch_shapes=[
                pltpu.VMEM((NX + 2, 3, 2, 32, L), F32),
                pltpu.VMEM((NX + 2, 3, 2, 32, L), F32),
                pltpu.VMEM((NX, 3, NY, L), F32),
                pltpu.VMEM((NX, 3, NY, L), F32),
                *[pltpu.VMEM((NA + 2 * EX, 4, 2, 32, L), F32)] * STAGES,
                *[pltpu.VMEM((NA, 4, NY, L), F32)] * STAGES,
                *[pltpu.VMEM((2, EX, 4, 2, NY, L), F32)] * STAGES,
                *[pltpu.VMEM((NA, 4, 2, NY, L), F32)] * STAGES,
                *[pltpu.VMEM((NA, 3, 2, NY, L), F32)] * 2,
                *[pltpu.VMEM((4, 2, 4, 3, NY, L), F32)] * 2,
                pltpu.VMEM((NA * NY * 8, L), F32),
                pltpu.VMEM((8 * 128, 6 * L), BF16),
                pltpu.VMEM((6, 768, 64), BF16),
                pltpu.VMEM((NA, NY, L), F32),
                pltpu.VMEM((8, 2, 64, 64), BF16),
                pltpu.VMEM((NA, NY), F32),
                pltpu.SemaphoreType.DMA((72,)),
                pltpu.SemaphoreType.DMA((72,)),
                pltpu.SemaphoreType.DMA((8,)),
            ],
            compiler_params=pltpu.CompilerParams(collective_id=0, has_side_effects=True, vmem_limit_bytes=60 << 20),
        )(les, mean_mach, transfer_tiles[:, 0], intersection_offset, state)
        return result.reshape(NA, NY, 2, 4, L).transpose(0, 1, 3, 2, 4).reshape(acoustic_state.shape)

    return jax.shard_map(body, mesh=mesh, in_specs=placed, out_specs=P("gx", "gy", None, "grp"), check_vma=False)
```

```python
import functools

import jax
import jax.numpy as jnp
from jax import lax
from jax.experimental import pallas as pl
from jax.experimental.pallas import tpu as pltpu
from jax.sharding import PartitionSpec as P

MESH = pl.DeviceIdType.MESH
F32, BF16 = jnp.float32, jnp.bfloat16

eddy_step = 0.1
viscosity = 0.5
wave_step = 0.2
filter_weight = 0.2
derivative_weights = (0.770882380518, -0.166705904415, 0.02084314277)
filter_taps = (0.28739284246, -0.226146951809, 0.10630357877, -0.023853048191)

NX, NA, NY, L = 32, 16, 16, 128
R0 = 8
EX = 3
STAGES = 6
QV, QP, QW, QU = 0, 1, 2, 3
ORDER = (QP, QU, QV, QW)
ROWS = pl.ds(R0, NY)


def kernel(count, les, mach, tiles, offs, state, out, *refs):
    (v0, v1, *zv), refs = refs[:4], refs[4:]
    f, zf, xh, yh, sb, refs = *(refs[k * STAGES:(k + 1) * STAGES] for k in range(4)), refs[4 * STAGES:4 * STAGES + 2], refs[4 * STAGES + 2:]
    s, tb, (stage, lb, wk, mb, tl, mc, send, recv, local) = refs[:2], refs[2:4], refs[4:]
    ix, iy, ig = lax.axis_index("gx"), lax.axis_index("gy"), lax.axis_index("grp")
    has_l, has_r = ix > 0, ix < count - 1
    right = {"gx": jnp.minimum(ix + 1, count - 1)}
    left = {"gx": jnp.maximum(ix - 1, 0)}
    side, twin = {"gy": 1 - iy}, {"grp": 1 - ig}
    later = ((ix == count // 2 - 1) | (ix == count // 2)) & (iy == 1)
    sooner = jnp.logical_not(later)

    bar = pltpu.get_barrier_semaphore()

    @pl.when(has_l)
    def _():
        pl.semaphore_signal(bar, inc=1, device_id=left, device_id_type=MESH)

    @pl.when(has_r)
    def _():
        pl.semaphore_signal(bar, inc=1, device_id=right, device_id_type=MESH)

    pl.semaphore_signal(bar, inc=1, device_id=side, device_id_type=MESH)
    pl.semaphore_signal(bar, inc=1, device_id=twin, device_id_type=MESH)

    loads = []
    for h in range(2):
        loads.append(pltpu.make_async_copy(les.at[:, :, :, pl.ds(L * h, L)], v0.at[pl.ds(1, NX), :, h, ROWS, :], local.at[h]))
    loads.append(pltpu.make_async_copy(state, stage, local.at[2]))
    loads.append(pltpu.make_async_copy(tiles, tl, local.at[3]))
    loads.append(pltpu.make_async_copy(mach, mc, local.at[4]))
    for c in loads:
        c.start()

    def clear(ref, width, always):
        n = ref.shape[0]

        def go(x, _):
            if always:
                for at in (0, 24):
                    ref[x, :, :, pl.ds(at, 8), :] = jnp.zeros(ref.shape[1:3] + (8, L), F32)
            else:
                at = pl.multiple_of(jnp.where(iy == 0, 0, 24), 8)
                ref[x, :, :, pl.ds(at, 8), :] = jnp.zeros(ref.shape[1:3] + (8, L), F32)
            return 0
        lax.fori_loop(width, n - width, go, 0)

        def ends(low):
            for x in range(width):
                ref[x if low else n - 1 - x, :, :, ROWS, :] = jnp.zeros(ref.shape[1:3] + (NY, L), F32)

        if always:
            ends(True)
            ends(False)
        else:
            pl.when(jnp.logical_not(has_l))(lambda: ends(True))
            pl.when(jnp.logical_not(has_r))(lambda: ends(False))

    def clear_rows(ref):
        def go(x, _):
            at = pl.multiple_of(8 * iy, 8)
            ref[x, :, :, pl.ds(at, 8), :] = jnp.zeros(ref.shape[1:3] + (8, L), F32)
            return 0
        lax.fori_loop(0, NA, go, 0)

    def remote(src, dst, to):
        k = remote.count
        remote.count += 1
        return pltpu.make_async_remote_copy(src, dst, send.at[k], recv.at[k], device_id=to, device_id_type=MESH)

    remote.count = 0
    sent = []

    class Sides:
        def __init__(self, pairs):
            self.low, self.high = [remote(*pairs[0], right)], [remote(*pairs[1], left)]
            sent.append(self)

        def start(self):
            pl.when(has_r)(self.low[0].start)
            pl.when(has_l)(self.high[0].start)

        def wait(self):
            pl.when(has_l)(self.low[0].wait_recv)
            pl.when(has_r)(self.high[0].wait_recv)

        def drain(self):
            pl.when(has_r)(self.low[0].wait_send)
            pl.when(has_l)(self.high[0].wait_send)

    class Cross:
        def __init__(self, ref, yref, zref, margin, width, x0, nx, all_fields):
            at, zat = pl.ds(margin + x0, nx), pl.ds(x0, nx)
            fy, fz = (slice(None),) * 2 if all_fields else (pl.ds(QV, 2), pl.ds(QP, 2))
            src = jnp.where(iy == 0, R0 + NY - width, R0)
            dst = jnp.where(iy == 0, R0 - width, R0 + NY)
            self.heard = False
            if yref is None:
                target = ref.at[at, fy, :, pl.ds(dst, width), :]
            else:
                target = yref.at[zat, fy, :, pl.ds(jnp.where(iy == 0, 8 - width, 8), width), :]
            self.side = remote(ref.at[at, fy, :, pl.ds(src, width), :], target, side)
            self.twin = remote(ref.at[at, fz, 1 - ig, ROWS, :], zref.at[zat, fz], twin)
            sent.append(self)

        def start(self):
            self.side.start()
            self.twin.start()

        def wait(self):
            self.wait_twin()
            self.wait_side()

        def wait_twin(self):
            self.twin.wait_recv()

        def wait_side(self):
            if self.heard:
                pl.when(sooner)(self.side.wait_recv)
            else:
                self.side.wait_recv()

        def hear(self):
            self.heard = True
            self.side.wait_recv()

        def drain(self):
            self.side.wait_send()
            self.twin.wait_send()

    def rims(n, h):
        half = slice(None) if h is None else h
        if n % 3 == 1:
            return Sides(((sb[n // 3].at[0, :, :, half], xh[n].at[0, :, :, half]), (sb[n // 3].at[1, :, :, half], xh[n].at[1, :, :, half])))
        return Sides(((f[n].at[pl.ds(EX + NA - EX, EX), :, half, ROWS, :], xh[n].at[0, :, :, half]),
                      (f[n].at[pl.ds(EX, EX), :, half, ROWS, :], xh[n].at[1, :, :, half])))

    def veil(v):
        return Sides(((v.at[pl.ds(NX, 1), :, :, ROWS, :], v.at[pl.ds(0, 1), :, :, ROWS, :]),
                      (v.at[pl.ds(1, 1), :, :, ROWS, :], v.at[pl.ds(NX + 1, 1), :, :, ROWS, :])))

    veils = [(veil(v), Cross(v, None, zv[n], 1, 1, 0, NX, True)) for n, v in enumerate((v0, v1))]
    sides, cross = [], []
    for n in range(STAGES):
        sides.append([rims(n, h) for h in range(2)])
        cuts = ((0, NA),) if n == 0 else ((4, 8), (0, 4), (12, 4)) if n % 3 == 1 else ((3, 10), (0, 3), (13, 3))
        cross.append([Cross(f[n], yh[n], zf[n], EX, EX, x0, nx, n in (2, 5)) for x0, nx in cuts])
    terms = [[Sides(((tb[n].at[3, h], tb[n].at[0, h]), (tb[n].at[2, h], tb[n].at[1, h]))) for h in range(2)] for n in range(2)]

    clear(v0, 1, False)
    loads[0].wait()
    loads[1].wait()
    pl.semaphore_wait(bar, 2 + has_l.astype(jnp.int32) + has_r.astype(jnp.int32))
    veils[0][0].start()
    veils[0][1].start()

    loads[2].wait()

    def relayout(x, _):
        for h in range(2):
            for c in range(4):
                f[0][x + EX, ORDER[c], h, ROWS, :] = stage[pl.ds(x * 128 + h * 4 + c, NY, stride=8), :]
        return 0

    lax.fori_loop(0, NA, relayout, 0)
    for h in range(2):
        sides[0][h].start()
    cross[0][0].start()
    clear(f[0], EX, True)
    clear_rows(yh[0])

    clear(v1, 1, False)
    for n in range(1, STAGES):
        clear(f[n], EX, True)
        clear_rows(yh[n])
    for n in range(2):
        @pl.when(jnp.logical_not(has_l))
        def _():
            tb[n][0] = jnp.zeros(tb[n].shape[1:], F32)

        @pl.when(jnp.logical_not(has_r))
        def _():
            tb[n][1] = jnp.zeros(tb[n].shape[1:], F32)

    loads[3].wait()
    loads[4].wait()

    flow = jnp.transpose(mc[...])
    for x in range(NA):
        mb[x] = jnp.broadcast_to(flow[:, x:x + 1], (NY, L))

    for m in range(-1, 5):
        for j in range(6):
            b = 2 * m - 2 + j
            if not 0 <= b < 8:
                continue
            if j in (2, 3):
                t = tl[b, 0]
            else:
                way = 1.0 if j < 2 else -1.0
                w = 0.5 + 0.5 * way * offs[b].astype(F32)
                t = (tl[b, 1].astype(F32) * w).astype(BF16)
            wk[m + 1, pl.ds(j * 128, 64), :] = t
            wk[m + 1, pl.ds(j * 128 + 64, 64), :] = t

    lane = lax.broadcasted_iota(jnp.int32, (NY, L), 1)
    keep = (lane >= 64).astype(jnp.int32) == ig

    def ahead(cur, nxt, j):
        return pltpu.roll(jnp.where(lane < j, nxt, cur), L - j, 1)

    def behind(cur, prv, j):
        return pltpu.roll(jnp.where(lane >= L - j, prv, cur), j, 1)

    def eddy(n, x):
        src, zsrc = (v0, v1)[n], zv[n]
        b, i = x // 4, lax.rem(x, 4)
        halves = [[src[x + 1, c, h, ROWS, :] for h in range(2)] for c in range(3)]
        edge = [jnp.where(keep, zsrc[x, c], 0.0) for c in range(3)]
        for h in range(2):
            grads, laps = [], []
            for c in range(3):
                cen = halves[c][h]
                xp, xm = src[x + 2, c, h, ROWS, :], src[x, c, h, ROWS, :]
                yp, ym = src[x + 1, c, h, pl.ds(R0 + 1, NY), :], src[x + 1, c, h, pl.ds(R0 - 1, NY), :]
                if n == 0 or c < 2:
                    nxt, prv = (halves[c][1], edge[c]) if h == 0 else (edge[c], halves[c][0])
                    zp, zm = ahead(cen, nxt, 1), behind(cen, prv, 1)
                else:
                    zp = zm = cen
                grads.append((0.5 * (xp - xm), 0.5 * (yp - ym), 0.5 * (zp - zm)))
                if n == 0:
                    laps.append(((xp + xm) + (yp + ym)) + ((zp + zm) - 6.0 * cen))
            u, v, w = (halves[c][h] for c in range(3))
            ox = grads[2][1] - grads[1][2]
            oy = grads[0][2] - grads[2][0]
            oz = grads[1][0] - grads[0][1]
            lamb = (oy * w - oz * v, oz * u - ox * w, ox * v - oy * u)
            for c in range(3):
                hi = lamb[c].astype(BF16)
                lo = (lamb[c] - hi.astype(F32)).astype(BF16)
                at = pl.multiple_of(b * 128 + i * 16, 16)
                lb[pl.ds(at, 16), pl.ds((h * 3 + c) * L, L)] = hi
                lb[pl.ds(at + 64, 16), pl.ds((h * 3 + c) * L, L)] = lo
                if n == 0:
                    v1[x + 1, c, h, ROWS, :] = halves[c][h] + eddy_step * (viscosity * laps[c] - lamb[c])

    def product(m, h=None):
        j0, j1 = max(0, 2 - 2 * m), min(6, 10 - 2 * m)
        rows = pl.ds((2 * m - 2 + j0) * 128, (j1 - j0) * 128)
        cols = pl.ds(0, 6 * L) if h is None else pl.ds(h * 3 * L, 3 * L)
        return lax.dot_general(wk[m + 1, pl.ds(j0 * 128, (j1 - j0) * 128), :], lb[rows, cols],
                               (((0,), (0,)), ((), ())), preferred_element_type=F32)

    def rim_terms(n, h):
        for m, slot in ((4, 3), (-1, 2)):
            r = product(m, h)
            for i in range(4):
                for c in range(3):
                    tb[n][slot, h, i, c] = r[i * 16:(i + 1) * 16, c * L:(c + 1) * L]

    def own_terms(n):
        for m in range(4):
            r = product(m)
            for i in range(4):
                for c in range(3):
                    for h in range(2):
                        s[n][4 * m + i, c, h] = r[i * 16:(i + 1) * 16, (h * 3 + c) * L:(h * 3 + c + 1) * L]

    def attach(n, h):
        for i in range(4):
            for c in range(3):
                s[n][i, c, h] = s[n][i, c, h] + tb[n][0, h, i, c]
                s[n][12 + i, c, h] = s[n][12 + i, c, h] + tb[n][1, h, i, c]

    def slope(ahead_, behind_):
        total = None
        for j in range(3):
            t = derivative_weights[j] * (ahead_[j] - behind_[j])
            total = t if total is None else total + t
        return total

    def beside(n, x, c, h):
        edge = jnp.where(keep, zf[n][x, c], 0.0)
        other = f[n][x + EX, c, 1 - h, ROWS, :]
        return (other, edge) if h == 0 else (edge, other)

    def rate(n, k, x, h):
        src = f[n]
        cen = [src[x + EX, c, h, ROWS, :] for c in range(4)]
        m = mb[x]

        def dx(c):
            return slope([src[x + EX + j, c, h, ROWS, :] for j in (1, 2, 3)], [src[x + EX - j, c, h, ROWS, :] for j in (1, 2, 3)])

        def dy(c):
            return slope([src[x + EX, c, h, pl.ds(R0 + j, NY), :] for j in (1, 2, 3)],
                         [src[x + EX, c, h, pl.ds(R0 - j, NY), :] for j in (1, 2, 3)])

        def dz(c):
            nxt, prv = beside(n, x, c, h)
            return slope([ahead(cen[c], nxt, j) for j in (1, 2, 3)], [behind(cen[c], prv, j) for j in (1, 2, 3)])

        d = [dx(c) for c in range(4)]
        r = [None] * 4
        r[QP] = -(m * d[QP] + d[QU] + dy(QV) + dz(QW))
        r[QU] = -(m * d[QU] + d[QP]) - s[k][x, 0, h]
        r[QV] = -(m * d[QV] + dy(QP)) - s[k][x, 1, h]
        r[QW] = -(m * d[QW] + dz(QP)) - s[k][x, 2, h]
        return cen, r

    def first(n, k, x, h):
        cen, r = rate(n, k, x, h)
        for c in range(4):
            f[n + 1][x + EX, c, h, ROWS, :] = cen[c] + wave_step * r[c]

    def second(n, k, x, h):
        cen, r = rate(n, k, x, h)
        for c in range(4):
            f[n + 1][x + EX, c, h, ROWS, :] = 0.5 * (f[n - 1][x + EX, c, h, ROWS, :] + cen[c]) + 0.5 * wave_step * r[c]

    def smooth(n, x, h):
        src = f[n]
        for q, c in enumerate(ORDER):
            cen = src[x + EX, c, h, ROWS, :]
            nxt, prv = beside(n, x, c, h)
            total = (1.0 - filter_weight * 3.0 * filter_taps[0]) * cen
            for j in (1, 2, 3):
                t = ((src[x + EX + j, c, h, ROWS, :] + src[x + EX - j, c, h, ROWS, :])
                     + (src[x + EX, c, h, pl.ds(R0 + j, NY), :] + src[x + EX, c, h, pl.ds(R0 - j, NY), :])
                     + (ahead(cen, nxt, j) + behind(cen, prv, j)))
                total = total - (filter_weight * filter_taps[j]) * t
            if n + 1 == STAGES:
                stage[pl.ds(x * 128 + h * 4 + q, NY, stride=8), :] = total
            else:
                f[n + 1][x + EX, c, h, ROWS, :] = total

    def correct_rows(n, x):
        kind = n % 3
        taps = [filter_weight * w for w in filter_taps[1:]] if kind == 2 else derivative_weights
        w = wave_step if kind == 0 else 0.5 * wave_step

        def side_of(low):
            own = 0 if low else 8
            for h in range(2):
                for c in range(4) if kind == 2 else (QV, QP):
                    total = None
                    for j in (1, 2, 3):
                        p = taps[j - 1] * yh[n][x, c, h, pl.ds(8 - j if low else j, 8), :]
                        total = p if total is None else total + p
                    to = c if kind == 2 else QP + QV - c
                    if n + 1 == STAGES:
                        at = pl.ds(x * 128 + own * 8 + h * 4 + ORDER.index(c), 8, stride=8)
                        stage[at, :] = stage[at, :] - total
                    else:
                        at = pl.ds(R0 + own, 8)
                        change = total if kind == 2 else (-w if low else w) * total
                        f[n + 1][x + EX, to, h, at, :] = f[n + 1][x + EX, to, h, at, :] - change

        pl.when(iy == 1)(lambda: side_of(True))
        pl.when(iy == 0)(lambda: side_of(False))

    def correct(n, h):
        kind = n % 3
        taps = [filter_weight * w for w in filter_taps[1:]] if kind == 2 else derivative_weights

        def side_of(low):
            halo = [[xh[n][0 if low else 1, EX - k if low else k - 1, c, h] for c in range(4)] for k in (1, 2, 3)]
            for i in range(EX):
                x = i if low else NA - 1 - i
                d = []
                for c in range(4):
                    total = taps[i] * halo[0][c]
                    for k in range(1, EX - i):
                        total = total + taps[i + k] * halo[k][c]
                    d.append(total)
                if kind == 2:
                    change = d
                else:
                    w = (wave_step if kind == 0 else 0.5 * wave_step) * (-1.0 if low else 1.0)
                    m = w * mb[x]
                    change = [None] * 4
                    change[QP] = m * d[QP] + w * d[QU]
                    change[QU] = m * d[QU] + w * d[QP]
                    change[QV] = m * d[QV]
                    change[QW] = m * d[QW]
                for q, c in enumerate(ORDER):
                    if n + 1 == STAGES:
                        at = pl.ds(x * 128 + h * 4 + q, NY, stride=8)
                        stage[at, :] = stage[at, :] - change[c]
                    else:
                        f[n + 1][x + EX, c, h, ROWS, :] = f[n + 1][x + EX, c, h, ROWS, :] - change[c]

        pl.when(has_l)(lambda: side_of(True))
        pl.when(has_r)(lambda: side_of(False))

    def over(lo, hi, step):
        def go(x, _):
            step(lo + 2 * x)
            step(lo + 2 * x + 1)
            return 0
        lax.fori_loop(0, (hi - lo) // 2, go, 0)

    def both(step):
        def go(x):
            step(x, 0)
            step(x, 1)
        return go

    def rim(width, step):
        def go(i):
            step(jnp.where(i < width, i, i + NA - 2 * width))
        over(0, 2 * width, go)

    def mend(k):
        n = 3 * k + 1
        for h in range(2):
            terms[k][h].wait()

            def go(i):
                for c, q in enumerate((QU, QV, QW)):
                    for x0, slot in ((0, 0), (12, 1)):
                        f[n][x0 + i + EX, q, h, ROWS, :] = f[n][x0 + i + EX, q, h, ROWS, :] - wave_step * tb[k][slot, h, i, c]
            over(0, 4, go)
        cross[n][1].start()
        cross[n][2].start()
        for h in range(2):
            attach(k, h)

    def mend_halo(k, h):
        n = 3 * k + 1
        for low, slot, first_layer in ((0, 2, 1), (1, 3, 0)):
            def go():
                for j in range(EX):
                    for c, q in enumerate((QU, QV, QW)):
                        xh[n][low, j, q, h] = xh[n][low, j, q, h] - wave_step * tb[k][slot, h, j + first_layer, c]
            pl.when(has_r if low else has_l)(go)

    veils[0][1].wait()
    over(1, NX - 1, functools.partial(eddy, 0))
    veils[0][0].wait()
    over(0, 2, lambda i: eddy(0, i * (NX - 1)))
    for h in range(2):
        rim_terms(0, h)
        terms[0][h].start()
    own_terms(0)

    for n in range(STAGES):
        step = (functools.partial(first, n, n // 3), functools.partial(second, n, n // 3), functools.partial(smooth, n))[n % 3]
        if n == 2:
            for c in veils[1]:
                c.wait()
            over(0, NX, functools.partial(eddy, 1))
            rim_terms(1, 0)
            terms[1][0].start()
            rim_terms(1, 1)
            own_terms(1)
        cross[n][0].wait_twin()
        if n == 0:
            over(0, NA, both(step))
        else:
            width = 4 if n % 3 == 1 else EX
            over(width, NA - width, both(step))
            cross[n][1].wait_twin()
            cross[n][2].wait_twin()
            rim(width, lambda x: both(step)(x))
        for c in cross[n]:
            c.wait_side()
        over(0, NA, functools.partial(correct_rows, n))
        if n + 1 == STAGES:
            inner = pltpu.make_async_copy(stage.at[pl.ds(3 * 128, 10 * 128)], out.at[pl.ds(3 * 128, 10 * 128)], local.at[0])
            inner.start()
        elif n % 3:
            cross[n + 1][0].start()
        for h in range(2):
            sides[n][h].wait()
            if n % 3 == 1:
                mend_halo(n // 3, h)
            correct(n, h)
            if n % 3 == 0:
                for j in range(EX):
                    for c in range(4):
                        sb[n // 3][0, j, c, h] = f[n + 1][EX + NA - EX + j, c, h, ROWS, :]
                        sb[n // 3][1, j, c, h] = f[n + 1][EX + j, c, h, ROWS, :]
            if n + 1 < STAGES:
                pl.when(sooner)(sides[n + 1][h].start)
        if n % 3 == 0:
            cross[n + 1][0].start()
        elif n + 1 < STAGES:
            cross[n + 1][1].start()
            cross[n + 1][2].start()
        if n + 1 < STAGES:
            @pl.when(later)
            def _():
                cross[n + 1][0 if n % 3 == 0 else 2].hear()
                for h in range(2):
                    sides[n + 1][h].start()
        if n % 3 == 0:
            mend(n // 3)
        if n == 0:
            for c in veils[1]:
                c.start()
        if n == 2:
            terms[1][1].start()
    outer = [pltpu.make_async_copy(stage.at[pl.ds(x * 128, 3 * 128)], out.at[pl.ds(x * 128, 3 * 128)], local.at[k])
             for k, x in ((1, 0), (2, 13))]
    for c in outer:
        c.start()
    for c in sent:
        c.drain()
    inner.wait()
    for c in outer:
        c.wait()


def solution(mesh):
    count = mesh.shape["gx"]
    placed = (
        P("gx", "gy", None, "grp"),
        P("gx", "gy"),
        P("gx", "gy", None, None, None),
        P("gx"),
        P("gx", "gy", None, "grp"),
    )

    def body(les_velocity, mean_mach, transfer_tiles, intersection_offset, acoustic_state):
        les = les_velocity.transpose(0, 2, 1, 3)
        state = acoustic_state.reshape(NA, NY, 4, 2, L).transpose(0, 1, 3, 2, 4).reshape(NA * NY * 8, L)
        anywhere = pl.BlockSpec(memory_space=pl.ANY)
        result = pl.pallas_call(
            functools.partial(kernel, count),
            out_shape=jax.ShapeDtypeStruct(state.shape, F32),
            in_specs=[anywhere, anywhere, anywhere, pl.BlockSpec(memory_space=pltpu.SMEM), anywhere],
            out_specs=anywhere,
            scratch_shapes=[
                pltpu.VMEM((NX + 2, 3, 2, 32, L), F32),
                pltpu.VMEM((NX + 2, 3, 2, 32, L), F32),
                pltpu.VMEM((NX, 3, NY, L), F32),
                pltpu.VMEM((NX, 3, NY, L), F32),
                *[pltpu.VMEM((NA + 2 * EX, 4, 2, 32, L), F32)] * STAGES,
                *[pltpu.VMEM((NA, 4, NY, L), F32)] * STAGES,
                *[pltpu.VMEM((2, EX, 4, 2, NY, L), F32)] * STAGES,
                *[pltpu.VMEM((NA, 4, 2, NY, L), F32)] * STAGES,
                *[pltpu.VMEM((2, EX, 4, 2, NY, L), F32)] * 2,
                *[pltpu.VMEM((NA, 3, 2, NY, L), F32)] * 2,
                *[pltpu.VMEM((4, 2, 4, 3, NY, L), F32)] * 2,
                pltpu.VMEM((NA * NY * 8, L), F32),
                pltpu.VMEM((8 * 128, 6 * L), BF16),
                pltpu.VMEM((6, 768, 64), BF16),
                pltpu.VMEM((NA, NY, L), F32),
                pltpu.VMEM((8, 2, 64, 64), BF16),
                pltpu.VMEM((NA, NY), F32),
                pltpu.SemaphoreType.DMA((72,)),
                pltpu.SemaphoreType.DMA((72,)),
                pltpu.SemaphoreType.DMA((8,)),
            ],
            compiler_params=pltpu.CompilerParams(collective_id=0, has_side_effects=True, vmem_limit_bytes=60 << 20),
        )(les, mean_mach, transfer_tiles[:, 0], intersection_offset, state)
        return result.reshape(NA, NY, 2, 4, L).transpose(0, 1, 3, 2, 4).reshape(acoustic_state.shape)

    return jax.shard_map(body, mesh=mesh, in_specs=placed, out_specs=P("gx", "gy", None, "grp"), check_vma=False)
```

```python
import functools

import jax
import jax.numpy as jnp
from jax import lax
from jax.experimental import pallas as pl
from jax.experimental.pallas import tpu as pltpu
from jax.sharding import PartitionSpec as P

MESH = pl.DeviceIdType.MESH
F32, BF16 = jnp.float32, jnp.bfloat16

eddy_step = 0.1
viscosity = 0.5
wave_step = 0.2
filter_weight = 0.2
derivative_weights = (0.770882380518, -0.166705904415, 0.02084314277)
filter_taps = (0.28739284246, -0.226146951809, 0.10630357877, -0.023853048191)

NX, NA, NY, L = 32, 16, 16, 128
R0 = 8
EX = 3
STAGES = 6
QV, QP, QW, QU = 0, 1, 2, 3
ORDER = (QP, QU, QV, QW)
ROWS = pl.ds(R0, NY)


def kernel(count, les, mach, tiles, offs, state, out, *refs):
    (v0, v1, *zv), refs = refs[:4], refs[4:]
    f, zf, xh, yh, sb, refs = *(refs[k * STAGES:(k + 1) * STAGES] for k in range(4)), refs[4 * STAGES:4 * STAGES + 2], refs[4 * STAGES + 2:]
    s, tb, (stage, lb, wk, mb, tl, mc, send, recv, local) = refs[:2], refs[2:4], refs[4:]
    ix, iy, ig = lax.axis_index("gx"), lax.axis_index("gy"), lax.axis_index("grp")
    has_l, has_r = ix > 0, ix < count - 1
    right = {"gx": jnp.minimum(ix + 1, count - 1)}
    left = {"gx": jnp.maximum(ix - 1, 0)}
    side, twin = {"gy": 1 - iy}, {"grp": 1 - ig}
    later = ((ix == count // 2 - 1) | (ix == count // 2)) & (iy == 1)
    sooner = jnp.logical_not(later)

    bar = pltpu.get_barrier_semaphore()

    @pl.when(has_l)
    def _():
        pl.semaphore_signal(bar, inc=1, device_id=left, device_id_type=MESH)

    @pl.when(has_r)
    def _():
        pl.semaphore_signal(bar, inc=1, device_id=right, device_id_type=MESH)

    pl.semaphore_signal(bar, inc=1, device_id=side, device_id_type=MESH)
    pl.semaphore_signal(bar, inc=1, device_id=twin, device_id_type=MESH)

    loads = []
    for h in range(2):
        loads.append(pltpu.make_async_copy(les.at[:, :, :, pl.ds(L * h, L)], v0.at[pl.ds(1, NX), :, h, ROWS, :], local.at[h]))
    loads.append(pltpu.make_async_copy(state, stage.at[pl.ds(0, NA * NY * 8)], local.at[2]))
    loads.append(pltpu.make_async_copy(tiles, tl, local.at[3]))
    loads.append(pltpu.make_async_copy(mach, mc, local.at[4]))
    for c in loads:
        c.start()

    def clear(ref, width, always):
        n = ref.shape[0]

        def go(x, _):
            if always:
                for at in (0, 24):
                    ref[x, :, :, pl.ds(at, 8), :] = jnp.zeros(ref.shape[1:3] + (8, L), F32)
            else:
                at = pl.multiple_of(jnp.where(iy == 0, 0, 24), 8)
                ref[x, :, :, pl.ds(at, 8), :] = jnp.zeros(ref.shape[1:3] + (8, L), F32)
            return 0
        lax.fori_loop(width, n - width, go, 0)

        def ends(low):
            for x in range(width):
                ref[x if low else n - 1 - x, :, :, ROWS, :] = jnp.zeros(ref.shape[1:3] + (NY, L), F32)

        if always:
            ends(True)
            ends(False)
        else:
            pl.when(jnp.logical_not(has_l))(lambda: ends(True))
            pl.when(jnp.logical_not(has_r))(lambda: ends(False))

    def clear_rows(ref):
        def go(x, _):
            at = pl.multiple_of(8 * iy, 8)
            ref[x, :, :, pl.ds(at, 8), :] = jnp.zeros(ref.shape[1:3] + (8, L), F32)
            return 0
        lax.fori_loop(0, NA, go, 0)

    def remote(src, dst, to):
        k = remote.count
        remote.count += 1
        return pltpu.make_async_remote_copy(src, dst, send.at[k], recv.at[k], device_id=to, device_id_type=MESH)

    remote.count = 0
    sent = []

    class Sides:
        def __init__(self, pairs):
            self.low, self.high = [remote(*pairs[0], right)], [remote(*pairs[1], left)]
            sent.append(self)

        def start(self):
            pl.when(has_r)(self.low[0].start)
            pl.when(has_l)(self.high[0].start)

        def wait(self):
            pl.when(has_l)(self.low[0].wait_recv)
            pl.when(has_r)(self.high[0].wait_recv)

        def drain(self):
            pl.when(has_r)(self.low[0].wait_send)
            pl.when(has_l)(self.high[0].wait_send)

    class Cross:
        def __init__(self, ref, yref, zref, margin, width, x0, nx, all_fields):
            at, zat = pl.ds(margin + x0, nx), pl.ds(x0, nx)
            fy, fz = (slice(None),) * 2 if all_fields else (pl.ds(QV, 2), pl.ds(QP, 2))
            src = jnp.where(iy == 0, R0 + NY - width, R0)
            dst = jnp.where(iy == 0, R0 - width, R0 + NY)
            self.heard = False
            if yref is None:
                target = ref.at[at, fy, :, pl.ds(dst, width), :]
            else:
                target = yref.at[zat, fy, :, pl.ds(jnp.where(iy == 0, 8 - width, 8), width), :]
            self.side = remote(ref.at[at, fy, :, pl.ds(src, width), :], target, side)
            self.twin = remote(ref.at[at, fz, 1 - ig, ROWS, :], zref.at[zat, fz], twin)
            sent.append(self)

        def start(self):
            self.side.start()
            self.twin.start()

        def wait(self):
            self.wait_twin()
            self.wait_side()

        def wait_twin(self):
            self.twin.wait_recv()

        def wait_side(self):
            if self.heard:
                pl.when(sooner)(self.side.wait_recv)
            else:
                self.side.wait_recv()

        def hear(self):
            self.heard = True
            self.side.wait_recv()

        def drain(self):
            self.side.wait_send()
            self.twin.wait_send()

    def rims(n, h):
        half = slice(None) if h is None else h
        if n % 3 == 1:
            return Sides(((sb[n // 3].at[0, :, :, half], xh[n].at[0, :, :, half]), (sb[n // 3].at[1, :, :, half], xh[n].at[1, :, :, half])))
        return Sides(((f[n].at[pl.ds(EX + NA - EX, EX), :, half, ROWS, :], xh[n].at[0, :, :, half]),
                      (f[n].at[pl.ds(EX, EX), :, half, ROWS, :], xh[n].at[1, :, :, half])))

    def veil(v):
        return Sides(((v.at[pl.ds(NX, 1), :, :, ROWS, :], v.at[pl.ds(0, 1), :, :, ROWS, :]),
                      (v.at[pl.ds(1, 1), :, :, ROWS, :], v.at[pl.ds(NX + 1, 1), :, :, ROWS, :])))

    veils = [(veil(v), Cross(v, None, zv[n], 1, 1, 0, NX, True)) for n, v in enumerate((v0, v1))]
    sides, cross = [], []
    for n in range(STAGES):
        sides.append([rims(n, h) for h in range(2)])
        cuts = ((0, NA),) if n == 0 else ((4, 8), (0, 4), (12, 4)) if n % 3 == 1 else ((3, 10), (0, 3), (13, 3))
        cross.append([Cross(f[n], yh[n], zf[n], EX, EX, x0, nx, n in (2, 5)) for x0, nx in cuts])
    terms = [[Sides(((tb[n].at[3, h], tb[n].at[0, h]), (tb[n].at[2, h], tb[n].at[1, h]))) for h in range(2)] for n in range(2)]

    clear(v0, 1, False)
    loads[0].wait()
    loads[1].wait()
    pl.semaphore_wait(bar, 2 + has_l.astype(jnp.int32) + has_r.astype(jnp.int32))
    veils[0][0].start()
    veils[0][1].start()

    loads[2].wait()

    def relayout(x, _):
        for h in range(2):
            for c in range(4):
                f[0][x + EX, ORDER[c], h, ROWS, :] = stage[pl.ds(x * 128 + h * 4 + c, NY, stride=8), :]
        return 0

    lax.fori_loop(0, NA, relayout, 0)
    for h in range(2):
        sides[0][h].start()
    cross[0][0].start()
    clear(f[0], EX, True)
    clear_rows(yh[0])

    clear(v1, 1, False)
    for n in range(1, STAGES):
        clear(f[n], EX, True)
        clear_rows(yh[n])
    for n in range(2):
        @pl.when(jnp.logical_not(has_l))
        def _():
            tb[n][0] = jnp.zeros(tb[n].shape[1:], F32)

        @pl.when(jnp.logical_not(has_r))
        def _():
            tb[n][1] = jnp.zeros(tb[n].shape[1:], F32)

    loads[3].wait()
    loads[4].wait()

    flow = jnp.transpose(mc[...])
    for x in range(NA):
        mb[x] = jnp.broadcast_to(flow[:, x:x + 1], (NY, L))

    for m in range(-1, 5):
        for j in range(6):
            b = 2 * m - 2 + j
            if not 0 <= b < 8:
                continue
            if j in (2, 3):
                t = tl[b, 0]
            else:
                way = 1.0 if j < 2 else -1.0
                w = 0.5 + 0.5 * way * offs[b].astype(F32)
                t = (tl[b, 1].astype(F32) * w).astype(BF16)
            wk[m + 1, pl.ds(j * 128, 64), :] = t
            wk[m + 1, pl.ds(j * 128 + 64, 64), :] = t

    lane = lax.broadcasted_iota(jnp.int32, (NY, L), 1)
    keep = (lane >= 64).astype(jnp.int32) == ig

    def ahead(cur, nxt, j):
        return pltpu.roll(jnp.where(lane < j, nxt, cur), L - j, 1)

    def behind(cur, prv, j):
        return pltpu.roll(jnp.where(lane >= L - j, prv, cur), j, 1)

    def eddy(n, x):
        src, zsrc = (v0, v1)[n], zv[n]
        b, i = x // 4, lax.rem(x, 4)
        halves = [[src[x + 1, c, h, ROWS, :] for h in range(2)] for c in range(3)]
        edge = [jnp.where(keep, zsrc[x, c], 0.0) for c in range(3)]
        for h in range(2):
            grads, laps = [], []
            for c in range(3):
                cen = halves[c][h]
                xp, xm = src[x + 2, c, h, ROWS, :], src[x, c, h, ROWS, :]
                yp, ym = src[x + 1, c, h, pl.ds(R0 + 1, NY), :], src[x + 1, c, h, pl.ds(R0 - 1, NY), :]
                if n == 0 or c < 2:
                    nxt, prv = (halves[c][1], edge[c]) if h == 0 else (edge[c], halves[c][0])
                    zp, zm = ahead(cen, nxt, 1), behind(cen, prv, 1)
                else:
                    zp = zm = cen
                grads.append((0.5 * (xp - xm), 0.5 * (yp - ym), 0.5 * (zp - zm)))
                if n == 0:
                    laps.append(((xp + xm) + (yp + ym)) + ((zp + zm) - 6.0 * cen))
            u, v, w = (halves[c][h] for c in range(3))
            ox = grads[2][1] - grads[1][2]
            oy = grads[0][2] - grads[2][0]
            oz = grads[1][0] - grads[0][1]
            lamb = (oy * w - oz * v, oz * u - ox * w, ox * v - oy * u)
            for c in range(3):
                hi = lamb[c].astype(BF16)
                lo = (lamb[c] - hi.astype(F32)).astype(BF16)
                at = pl.multiple_of(b * 128 + i * 16, 16)
                lb[pl.ds(at, 16), pl.ds((h * 3 + c) * L, L)] = hi
                lb[pl.ds(at + 64, 16), pl.ds((h * 3 + c) * L, L)] = lo
                if n == 0:
                    v1[x + 1, c, h, ROWS, :] = halves[c][h] + eddy_step * (viscosity * laps[c] - lamb[c])

    def product(m, h=None):
        j0, j1 = max(0, 2 - 2 * m), min(6, 10 - 2 * m)
        rows = pl.ds((2 * m - 2 + j0) * 128, (j1 - j0) * 128)
        cols = pl.ds(0, 6 * L) if h is None else pl.ds(h * 3 * L, 3 * L)
        return lax.dot_general(wk[m + 1, pl.ds(j0 * 128, (j1 - j0) * 128), :], lb[rows, cols],
                               (((0,), (0,)), ((), ())), preferred_element_type=F32)

    def rim_terms(n, h):
        for m, slot in ((4, 3), (-1, 2)):
            r = product(m, h)
            for i in range(4):
                for c in range(3):
                    tb[n][slot, h, i, c] = r[i * 16:(i + 1) * 16, c * L:(c + 1) * L]

    def own_terms(n):
        for m in range(4):
            r = product(m)
            for i in range(4):
                for c in range(3):
                    for h in range(2):
                        s[n][4 * m + i, c, h] = r[i * 16:(i + 1) * 16, (h * 3 + c) * L:(h * 3 + c + 1) * L]

    def attach(n, h):
        for i in range(4):
            for c in range(3):
                s[n][i, c, h] = s[n][i, c, h] + tb[n][0, h, i, c]
                s[n][12 + i, c, h] = s[n][12 + i, c, h] + tb[n][1, h, i, c]

    def slope(ahead_, behind_):
        total = None
        for j in range(3):
            t = derivative_weights[j] * (ahead_[j] - behind_[j])
            total = t if total is None else total + t
        return total

    def beside(n, x, c, h):
        edge = jnp.where(keep, zf[n][x, c], 0.0)
        other = f[n][x + EX, c, 1 - h, ROWS, :]
        return (other, edge) if h == 0 else (edge, other)

    def rate(n, k, x, h):
        src = f[n]
        cen = [src[x + EX, c, h, ROWS, :] for c in range(4)]
        m = mb[x]

        def dx(c):
            return slope([src[x + EX + j, c, h, ROWS, :] for j in (1, 2, 3)], [src[x + EX - j, c, h, ROWS, :] for j in (1, 2, 3)])

        def dy(c):
            return slope([src[x + EX, c, h, pl.ds(R0 + j, NY), :] for j in (1, 2, 3)],
                         [src[x + EX, c, h, pl.ds(R0 - j, NY), :] for j in (1, 2, 3)])

        def dz(c):
            nxt, prv = beside(n, x, c, h)
            return slope([ahead(cen[c], nxt, j) for j in (1, 2, 3)], [behind(cen[c], prv, j) for j in (1, 2, 3)])

        d = [dx(c) for c in range(4)]
        r = [None] * 4
        r[QP] = -(m * d[QP] + d[QU] + dy(QV) + dz(QW))
        r[QU] = -(m * d[QU] + d[QP]) - s[k][x, 0, h]
        r[QV] = -(m * d[QV] + dy(QP)) - s[k][x, 1, h]
        r[QW] = -(m * d[QW] + dz(QP)) - s[k][x, 2, h]
        return cen, r

    def first(n, k, x, h):
        cen, r = rate(n, k, x, h)
        for c in range(4):
            f[n + 1][x + EX, c, h, ROWS, :] = cen[c] + wave_step * r[c]

    def second(n, k, x, h):
        cen, r = rate(n, k, x, h)
        for c in range(4):
            f[n + 1][x + EX, c, h, ROWS, :] = 0.5 * (f[n - 1][x + EX, c, h, ROWS, :] + cen[c]) + 0.5 * wave_step * r[c]

    def smooth(n, x, h):
        src = f[n]
        for q, c in enumerate(ORDER):
            cen = src[x + EX, c, h, ROWS, :]
            nxt, prv = beside(n, x, c, h)
            total = (1.0 - filter_weight * 3.0 * filter_taps[0]) * cen
            for j in (1, 2, 3):
                t = ((src[x + EX + j, c, h, ROWS, :] + src[x + EX - j, c, h, ROWS, :])
                     + (src[x + EX, c, h, pl.ds(R0 + j, NY), :] + src[x + EX, c, h, pl.ds(R0 - j, NY), :])
                     + (ahead(cen, nxt, j) + behind(cen, prv, j)))
                total = total - (filter_weight * filter_taps[j]) * t
            if n + 1 == STAGES:
                stage[pl.ds(x * 128 + h * 4 + q, NY, stride=8), :] = total
            else:
                f[n + 1][x + EX, c, h, ROWS, :] = total

    def correct_rows(n, x):
        kind = n % 3
        taps = [filter_weight * w for w in filter_taps[1:]] if kind == 2 else derivative_weights
        w = wave_step if kind == 0 else 0.5 * wave_step

        def side_of(low):
            own = 0 if low else 8
            for h in range(2):
                for c in range(4) if kind == 2 else (QV, QP):
                    total = None
                    for j in (1, 2, 3):
                        p = taps[j - 1] * yh[n][x, c, h, pl.ds(8 - j if low else j, 8), :]
                        total = p if total is None else total + p
                    to = c if kind == 2 else QP + QV - c
                    if n + 1 == STAGES:
                        at = pl.ds(x * 128 + own * 8 + h * 4 + ORDER.index(c), 8, stride=8)
                        stage[at, :] = stage[at, :] - total
                    else:
                        at = pl.ds(R0 + own, 8)
                        change = total if kind == 2 else (-w if low else w) * total
                        f[n + 1][x + EX, to, h, at, :] = f[n + 1][x + EX, to, h, at, :] - change

        pl.when(iy == 1)(lambda: side_of(True))
        pl.when(iy == 0)(lambda: side_of(False))

    def correct(n, h):
        kind = n % 3
        taps = [filter_weight * w for w in filter_taps[1:]] if kind == 2 else derivative_weights

        def side_of(low):
            halo = [[xh[n][0 if low else 1, EX - k if low else k - 1, c, h] for c in range(4)] for k in (1, 2, 3)]
            for i in range(EX):
                x = i if low else NA - 1 - i
                d = []
                for c in range(4):
                    total = taps[i] * halo[0][c]
                    for k in range(1, EX - i):
                        total = total + taps[i + k] * halo[k][c]
                    d.append(total)
                if kind == 2:
                    change = d
                else:
                    w = (wave_step if kind == 0 else 0.5 * wave_step) * (-1.0 if low else 1.0)
                    m = w * mb[x]
                    change = [None] * 4
                    change[QP] = m * d[QP] + w * d[QU]
                    change[QU] = m * d[QU] + w * d[QP]
                    change[QV] = m * d[QV]
                    change[QW] = m * d[QW]
                for q, c in enumerate(ORDER):
                    if n + 1 == STAGES:
                        at = pl.ds(x * 128 + h * 4 + q, NY, stride=8)
                        stage[at, :] = stage[at, :] - change[c]
                    else:
                        f[n + 1][x + EX, c, h, ROWS, :] = f[n + 1][x + EX, c, h, ROWS, :] - change[c]

        pl.when(has_l)(lambda: side_of(True))
        pl.when(has_r)(lambda: side_of(False))

    def over(lo, hi, step):
        def go(x, _):
            step(lo + 2 * x)
            step(lo + 2 * x + 1)
            return 0
        lax.fori_loop(0, (hi - lo) // 2, go, 0)

    def both(step):
        def go(x):
            step(x, 0)
            step(x, 1)
        return go

    def rim(width, step):
        def go(i):
            step(jnp.where(i < width, i, i + NA - 2 * width))
        over(0, 2 * width, go)

    def mend(k):
        n = 3 * k + 1
        for h in range(2):
            terms[k][h].wait()

            def go(i):
                for c, q in enumerate((QU, QV, QW)):
                    for x0, slot in ((0, 0), (12, 1)):
                        f[n][x0 + i + EX, q, h, ROWS, :] = f[n][x0 + i + EX, q, h, ROWS, :] - wave_step * tb[k][slot, h, i, c]
            over(0, 4, go)
        cross[n][1].start()
        cross[n][2].start()
        for h in range(2):
            attach(k, h)

    def mend_halo(k, h):
        n = 3 * k + 1
        for low, slot, first_layer in ((0, 2, 1), (1, 3, 0)):
            def go():
                for j in range(EX):
                    for c, q in enumerate((QU, QV, QW)):
                        xh[n][low, j, q, h] = xh[n][low, j, q, h] - wave_step * tb[k][slot, h, j + first_layer, c]
            pl.when(has_r if low else has_l)(go)

    veils[0][1].wait()
    over(1, NX - 1, functools.partial(eddy, 0))
    veils[0][0].wait()
    over(0, 2, lambda i: eddy(0, i * (NX - 1)))
    for h in range(2):
        rim_terms(0, h)
        terms[0][h].start()
    own_terms(0)

    for n in range(STAGES):
        step = (functools.partial(first, n, n // 3), functools.partial(second, n, n // 3), functools.partial(smooth, n))[n % 3]
        if n == 2:
            for c in veils[1]:
                c.wait()
            over(0, NX, functools.partial(eddy, 1))
            rim_terms(1, 0)
            terms[1][0].start()
            rim_terms(1, 1)
            own_terms(1)
        cross[n][0].wait_twin()
        if n == 0:
            over(0, NA, both(step))
        else:
            width = 4 if n % 3 == 1 else EX
            over(width, NA - width, both(step))
            cross[n][1].wait_twin()
            cross[n][2].wait_twin()
            rim(width, lambda x: both(step)(x))
        for c in cross[n]:
            c.wait_side()
        over(0, NA, functools.partial(correct_rows, n))
        if n + 1 == STAGES:
            inner = pltpu.make_async_copy(stage.at[pl.ds(3 * 128, 10 * 128)], out.at[pl.ds(3 * 128, 10 * 128)], local.at[0])
            inner.start()
        elif n % 3:
            cross[n + 1][0].start()
        for h in range(2):
            sides[n][h].wait()
            if n % 3 == 1:
                mend_halo(n // 3, h)
            correct(n, h)
            if n % 3 == 0:
                for j in range(EX):
                    for c in range(4):
                        sb[n // 3][0, j, c, h] = f[n + 1][EX + NA - EX + j, c, h, ROWS, :]
                        sb[n // 3][1, j, c, h] = f[n + 1][EX + j, c, h, ROWS, :]
            if n + 1 < STAGES:
                pl.when(sooner)(sides[n + 1][h].start)
        if n % 3 == 0:
            cross[n + 1][0].start()
        elif n + 1 < STAGES:
            cross[n + 1][1].start()
            cross[n + 1][2].start()
        if n + 1 < STAGES:
            @pl.when(later)
            def _():
                cross[n + 1][0 if n % 3 == 0 else 2].hear()
                for h in range(2):
                    sides[n + 1][h].start()
        if n % 3 == 0:
            mend(n // 3)
        if n == 0:
            for c in veils[1]:
                c.start()
        if n == 2:
            terms[1][1].start()
    outer = [pltpu.make_async_copy(stage.at[pl.ds(x * 128, 3 * 128)], out.at[pl.ds(x * 128, 3 * 128)], local.at[k])
             for k, x in ((1, 0), (2, 13))]
    for c in outer:
        c.start()
    for c in sent:
        c.drain()
    inner.wait()
    for c in outer:
        c.wait()


def solution(mesh):
    count = mesh.shape["gx"]
    placed = (
        P("gx", "gy", None, "grp"),
        P("gx", "gy"),
        P("gx", "gy", None, None, None),
        P("gx"),
        P("gx", "gy", None, "grp"),
    )

    def body(les_velocity, mean_mach, transfer_tiles, intersection_offset, acoustic_state):
        les = les_velocity.transpose(0, 2, 1, 3)
        state = acoustic_state.reshape(NA, NY, 4, 2, L).transpose(0, 1, 3, 2, 4).reshape(NA * NY * 8, L)
        anywhere = pl.BlockSpec(memory_space=pl.ANY)
        result = pl.pallas_call(
            functools.partial(kernel, count),
            out_shape=jax.ShapeDtypeStruct(state.shape, F32),
            in_specs=[anywhere, anywhere, anywhere, pl.BlockSpec(memory_space=pltpu.SMEM), anywhere],
            out_specs=anywhere,
            scratch_shapes=[
                pltpu.VMEM((NX + 2, 3, 2, 32, L), F32),
                pltpu.VMEM((NX + 2, 3, 2, 32, L), F32),
                pltpu.VMEM((NX, 3, NY, L), F32),
                pltpu.VMEM((NX, 3, NY, L), F32),
                *[pltpu.VMEM((NA + 2 * EX, 4, 2, 32, L), F32)] * STAGES,
                *[pltpu.VMEM((NA, 4, NY, L), F32)] * STAGES,
                *[pltpu.VMEM((2, EX, 4, 2, NY, L), F32)] * STAGES,
                *[pltpu.VMEM((NA, 4, 2, NY, L), F32)] * STAGES,
                *[pltpu.VMEM((2, EX, 4, 2, NY, L), F32)] * 2,
                *[pltpu.VMEM((NA, 3, 2, NY, L), F32)] * 2,
                *[pltpu.VMEM((4, 2, 4, 3, NY, L), F32)] * 2,
                pltpu.VMEM((NA * NY * 8 + 8, L), F32),
                pltpu.VMEM((8 * 128, 6 * L), BF16),
                pltpu.VMEM((6, 768, 64), BF16),
                pltpu.VMEM((NA, NY, L), F32),
                pltpu.VMEM((8, 2, 64, 64), BF16),
                pltpu.VMEM((NA, NY), F32),
                pltpu.SemaphoreType.DMA((72,)),
                pltpu.SemaphoreType.DMA((72,)),
                pltpu.SemaphoreType.DMA((8,)),
            ],
            compiler_params=pltpu.CompilerParams(collective_id=0, has_side_effects=True, vmem_limit_bytes=60 << 20),
        )(les, mean_mach, transfer_tiles[:, 0], intersection_offset, state)
        return result.reshape(NA, NY, 2, 4, L).transpose(0, 1, 3, 2, 4).reshape(acoustic_state.shape)

    return jax.shard_map(body, mesh=mesh, in_specs=placed, out_specs=P("gx", "gy", None, "grp"), check_vma=False)
```

```python
import functools

import jax
import jax.numpy as jnp
from jax import lax
from jax.experimental import pallas as pl
from jax.experimental.pallas import tpu as pltpu
from jax.sharding import PartitionSpec as P

MESH = pl.DeviceIdType.MESH
F32, BF16 = jnp.float32, jnp.bfloat16

eddy_step = 0.1
viscosity = 0.5
wave_step = 0.2
filter_weight = 0.2
derivative_weights = (0.770882380518, -0.166705904415, 0.02084314277)
filter_taps = (0.28739284246, -0.226146951809, 0.10630357877, -0.023853048191)

NX, NA, NY, L = 32, 16, 16, 128
R0 = 8
EX = 3
STAGES = 6
QV, QP, QW, QU = 0, 1, 2, 3
ORDER = (QP, QU, QV, QW)
ROWS = pl.ds(R0, NY)


def kernel(count, les, mach, tiles, offs, state, out, *refs):
    (v0, v1, *zv), refs = refs[:4], refs[4:]
    f, zf, xh, yh, sb, refs = *(refs[k * STAGES:(k + 1) * STAGES] for k in range(4)), refs[4 * STAGES:4 * STAGES + 2], refs[4 * STAGES + 2:]
    s, tb, (stage, lb, wk, mb, tl, mc, send, recv, local) = refs[:2], refs[2:4], refs[4:]
    ix, iy, ig = lax.axis_index("gx"), lax.axis_index("gy"), lax.axis_index("grp")
    has_l, has_r = ix > 0, ix < count - 1
    right = {"gx": jnp.minimum(ix + 1, count - 1)}
    left = {"gx": jnp.maximum(ix - 1, 0)}
    side, twin = {"gy": 1 - iy}, {"grp": 1 - ig}
    later = ((ix == count // 2 - 1) | (ix == count // 2)) & (iy == 1)
    sooner = jnp.logical_not(later)

    bar = pltpu.get_barrier_semaphore()

    @pl.when(has_l)
    def _():
        pl.semaphore_signal(bar, inc=1, device_id=left, device_id_type=MESH)

    @pl.when(has_r)
    def _():
        pl.semaphore_signal(bar, inc=1, device_id=right, device_id_type=MESH)

    pl.semaphore_signal(bar, inc=1, device_id=side, device_id_type=MESH)
    pl.semaphore_signal(bar, inc=1, device_id=twin, device_id_type=MESH)

    loads = []
    for h in range(2):
        loads.append(pltpu.make_async_copy(les.at[:, :, :, pl.ds(L * h, L)], v0.at[pl.ds(1, NX), :, h, ROWS, :], local.at[h]))
    loads.append(pltpu.make_async_copy(state, stage.at[pl.ds(0, NA * NY * 8)], local.at[2]))
    loads.append(pltpu.make_async_copy(tiles, tl, local.at[3]))
    loads.append(pltpu.make_async_copy(mach, mc, local.at[4]))
    for c in loads:
        c.start()

    def clear(ref, width, always):
        n = ref.shape[0]

        def go(x, _):
            if always:
                for at in (0, 24):
                    ref[x, :, :, pl.ds(at, 8), :] = jnp.zeros(ref.shape[1:3] + (8, L), F32)
            else:
                at = pl.multiple_of(jnp.where(iy == 0, 0, 24), 8)
                ref[x, :, :, pl.ds(at, 8), :] = jnp.zeros(ref.shape[1:3] + (8, L), F32)
            return 0
        lax.fori_loop(width, n - width, go, 0)

        def ends(low):
            for x in range(width):
                ref[x if low else n - 1 - x, :, :, ROWS, :] = jnp.zeros(ref.shape[1:3] + (NY, L), F32)

        if always:
            ends(True)
            ends(False)
        else:
            pl.when(jnp.logical_not(has_l))(lambda: ends(True))
            pl.when(jnp.logical_not(has_r))(lambda: ends(False))

    def clear_rows(ref):
        def go(x, _):
            at = pl.multiple_of(8 * iy, 8)
            ref[x, :, :, pl.ds(at, 8), :] = jnp.zeros(ref.shape[1:3] + (8, L), F32)
            return 0
        lax.fori_loop(0, NA, go, 0)

    def remote(src, dst, to):
        k = remote.count
        remote.count += 1
        return pltpu.make_async_remote_copy(src, dst, send.at[k], recv.at[k], device_id=to, device_id_type=MESH)

    remote.count = 0
    sent = []

    class Sides:
        def __init__(self, pairs):
            self.low, self.high = [remote(*pairs[0], right)], [remote(*pairs[1], left)]
            sent.append(self)

        def start(self):
            pl.when(has_r)(self.low[0].start)
            pl.when(has_l)(self.high[0].start)

        def wait(self):
            pl.when(has_l)(self.low[0].wait_recv)
            pl.when(has_r)(self.high[0].wait_recv)

        def drain(self):
            pl.when(has_r)(self.low[0].wait_send)
            pl.when(has_l)(self.high[0].wait_send)

    class Cross:
        def __init__(self, ref, yref, zref, margin, width, x0, nx, all_fields):
            at, zat = pl.ds(margin + x0, nx), pl.ds(x0, nx)
            fy, fz = (slice(None),) * 2 if all_fields else (pl.ds(QV, 2), pl.ds(QP, 2))
            src = jnp.where(iy == 0, R0 + NY - width, R0)
            dst = jnp.where(iy == 0, R0 - width, R0 + NY)
            self.heard = False
            if yref is None:
                target = ref.at[at, fy, :, pl.ds(dst, width), :]
            else:
                target = yref.at[zat, fy, :, pl.ds(jnp.where(iy == 0, 8 - width, 8), width), :]
            self.side = remote(ref.at[at, fy, :, pl.ds(src, width), :], target, side)
            self.twin = remote(ref.at[at, fz, 1 - ig, ROWS, :], zref.at[zat, fz], twin)
            sent.append(self)

        def start(self):
            self.side.start()
            self.twin.start()

        def wait(self):
            self.wait_twin()
            self.wait_side()

        def wait_twin(self):
            self.twin.wait_recv()

        def wait_side(self):
            if self.heard:
                pl.when(sooner)(self.side.wait_recv)
            else:
                self.side.wait_recv()

        def hear(self):
            self.heard = True
            self.side.wait_recv()

        def drain(self):
            self.side.wait_send()
            self.twin.wait_send()

    def rims(n, h):
        half = slice(None) if h is None else h
        if n % 3 == 1:
            return Sides(((sb[n // 3].at[0, :, :, half], xh[n].at[0, :, :, half]), (sb[n // 3].at[1, :, :, half], xh[n].at[1, :, :, half])))
        return Sides(((f[n].at[pl.ds(EX + NA - EX, EX), :, half, ROWS, :], xh[n].at[0, :, :, half]),
                      (f[n].at[pl.ds(EX, EX), :, half, ROWS, :], xh[n].at[1, :, :, half])))

    def veil(v):
        return Sides(((v.at[pl.ds(NX, 1), :, :, ROWS, :], v.at[pl.ds(0, 1), :, :, ROWS, :]),
                      (v.at[pl.ds(1, 1), :, :, ROWS, :], v.at[pl.ds(NX + 1, 1), :, :, ROWS, :])))

    veils = [(veil(v), Cross(v, None, zv[n], 1, 1, 0, NX, True)) for n, v in enumerate((v0, v1))]
    sides, cross = [], []
    for n in range(STAGES):
        sides.append([rims(n, h) for h in range(2)])
        cuts = ((0, NA),) if n == 0 else ((4, 8), (0, 4), (12, 4)) if n % 3 == 1 else ((3, 10), (0, 3), (13, 3))
        cross.append([Cross(f[n], yh[n], zf[n], EX, EX, x0, nx, n in (2, 5)) for x0, nx in cuts])
    terms = [[Sides(((tb[n].at[3, h], tb[n].at[0, h]), (tb[n].at[2, h], tb[n].at[1, h]))) for h in range(2)] for n in range(2)]

    clear(v0, 1, False)
    loads[0].wait()
    loads[1].wait()
    pl.semaphore_wait(bar, 2 + has_l.astype(jnp.int32) + has_r.astype(jnp.int32))
    veils[0][0].start()
    veils[0][1].start()

    loads[2].wait()

    def relayout(x, _):
        for h in range(2):
            for c in range(4):
                f[0][x + EX, ORDER[c], h, ROWS, :] = stage[pl.ds(x * 128 + h * 4 + c, NY, stride=8), :]
        return 0

    lax.fori_loop(0, NA, relayout, 0)
    for h in range(2):
        sides[0][h].start()
    cross[0][0].start()
    clear(f[0], EX, True)
    clear_rows(yh[0])

    clear(v1, 1, False)
    for n in range(1, STAGES):
        clear(f[n], EX, True)
        clear_rows(yh[n])
    for n in range(2):
        @pl.when(jnp.logical_not(has_l))
        def _():
            tb[n][0] = jnp.zeros(tb[n].shape[1:], F32)

        @pl.when(jnp.logical_not(has_r))
        def _():
            tb[n][1] = jnp.zeros(tb[n].shape[1:], F32)

    loads[3].wait()
    loads[4].wait()

    flow = jnp.transpose(mc[...])
    for x in range(NA):
        mb[x] = jnp.broadcast_to(flow[:, x:x + 1], (NY, L))

    for m in range(-1, 5):
        for j in range(6):
            b = 2 * m - 2 + j
            if not 0 <= b < 8:
                continue
            if j in (2, 3):
                t = tl[b, 0]
            else:
                way = 1.0 if j < 2 else -1.0
                w = 0.5 + 0.5 * way * offs[b].astype(F32)
                t = (tl[b, 1].astype(F32) * w).astype(BF16)
            wk[m + 1, pl.ds(j * 128, 64), :] = t
            wk[m + 1, pl.ds(j * 128 + 64, 64), :] = t

    lane = lax.broadcasted_iota(jnp.int32, (NY, L), 1)
    keep = (lane >= 64).astype(jnp.int32) == ig

    def ahead(cur, nxt, j):
        return pltpu.roll(jnp.where(lane < j, nxt, cur), L - j, 1)

    def behind(cur, prv, j):
        return pltpu.roll(jnp.where(lane >= L - j, prv, cur), j, 1)

    def eddy(n, x):
        src, zsrc = (v0, v1)[n], zv[n]
        b, i = x // 4, lax.rem(x, 4)
        halves = [[src[x + 1, c, h, ROWS, :] for h in range(2)] for c in range(3)]
        edge = [jnp.where(keep, zsrc[x, c], 0.0) for c in range(3)]
        for h in range(2):
            grads, laps = [], []
            for c in range(3):
                cen = halves[c][h]
                xp, xm = src[x + 2, c, h, ROWS, :], src[x, c, h, ROWS, :]
                yp, ym = src[x + 1, c, h, pl.ds(R0 + 1, NY), :], src[x + 1, c, h, pl.ds(R0 - 1, NY), :]
                if n == 0 or c < 2:
                    nxt, prv = (halves[c][1], edge[c]) if h == 0 else (edge[c], halves[c][0])
                    zp, zm = ahead(cen, nxt, 1), behind(cen, prv, 1)
                else:
                    zp = zm = cen
                grads.append((0.5 * (xp - xm), 0.5 * (yp - ym), 0.5 * (zp - zm)))
                if n == 0:
                    laps.append(((xp + xm) + (yp + ym)) + ((zp + zm) - 6.0 * cen))
            u, v, w = (halves[c][h] for c in range(3))
            ox = grads[2][1] - grads[1][2]
            oy = grads[0][2] - grads[2][0]
            oz = grads[1][0] - grads[0][1]
            lamb = (oy * w - oz * v, oz * u - ox * w, ox * v - oy * u)
            for c in range(3):
                hi = lamb[c].astype(BF16)
                lo = (lamb[c] - hi.astype(F32)).astype(BF16)
                at = pl.multiple_of(b * 128 + i * 16, 16)
                lb[pl.ds(at, 16), pl.ds((h * 3 + c) * L, L)] = hi
                lb[pl.ds(at + 64, 16), pl.ds((h * 3 + c) * L, L)] = lo
                if n == 0:
                    v1[x + 1, c, h, ROWS, :] = halves[c][h] + eddy_step * (viscosity * laps[c] - lamb[c])

    def product(m, h=None):
        j0, j1 = max(0, 2 - 2 * m), min(6, 10 - 2 * m)
        rows = pl.ds((2 * m - 2 + j0) * 128, (j1 - j0) * 128)
        cols = pl.ds(0, 6 * L) if h is None else pl.ds(h * 3 * L, 3 * L)
        return lax.dot_general(wk[m + 1, pl.ds(j0 * 128, (j1 - j0) * 128), :], lb[rows, cols],
                               (((0,), (0,)), ((), ())), preferred_element_type=F32)

    def rim_terms(n, h):
        for m, slot in ((4, 3), (-1, 2)):
            r = product(m, h)
            for i in range(4):
                for c in range(3):
                    tb[n][slot, h, i, c] = r[i * 16:(i + 1) * 16, c * L:(c + 1) * L]

    def own_terms(n):
        for m in range(4):
            r = product(m)
            for i in range(4):
                for c in range(3):
                    for h in range(2):
                        s[n][4 * m + i, c, h] = r[i * 16:(i + 1) * 16, (h * 3 + c) * L:(h * 3 + c + 1) * L]

    def attach(n, h):
        for i in range(4):
            for c in range(3):
                s[n][i, c, h] = s[n][i, c, h] + tb[n][0, h, i, c]
                s[n][12 + i, c, h] = s[n][12 + i, c, h] + tb[n][1, h, i, c]

    def slope(ahead_, behind_):
        total = None
        for j in range(3):
            t = derivative_weights[j] * (ahead_[j] - behind_[j])
            total = t if total is None else total + t
        return total

    def beside(n, x, c, h):
        edge = jnp.where(keep, zf[n][x, c], 0.0)
        other = f[n][x + EX, c, 1 - h, ROWS, :]
        return (other, edge) if h == 0 else (edge, other)

    def rate(n, k, x, h):
        src = f[n]
        cen = [src[x + EX, c, h, ROWS, :] for c in range(4)]
        m = mb[x]

        def dx(c):
            return slope([src[x + EX + j, c, h, ROWS, :] for j in (1, 2, 3)], [src[x + EX - j, c, h, ROWS, :] for j in (1, 2, 3)])

        def dy(c):
            return slope([src[x + EX, c, h, pl.ds(R0 + j, NY), :] for j in (1, 2, 3)],
                         [src[x + EX, c, h, pl.ds(R0 - j, NY), :] for j in (1, 2, 3)])

        def dz(c):
            nxt, prv = beside(n, x, c, h)
            return slope([ahead(cen[c], nxt, j) for j in (1, 2, 3)], [behind(cen[c], prv, j) for j in (1, 2, 3)])

        d = [dx(c) for c in range(4)]
        r = [None] * 4
        r[QP] = -(m * d[QP] + d[QU] + dy(QV) + dz(QW))
        r[QU] = -(m * d[QU] + d[QP]) - s[k][x, 0, h]
        r[QV] = -(m * d[QV] + dy(QP)) - s[k][x, 1, h]
        r[QW] = -(m * d[QW] + dz(QP)) - s[k][x, 2, h]
        return cen, r

    def first(n, k, x, h):
        cen, r = rate(n, k, x, h)
        for c in range(4):
            f[n + 1][x + EX, c, h, ROWS, :] = cen[c] + wave_step * r[c]

    def second(n, k, x, h):
        cen, r = rate(n, k, x, h)
        for c in range(4):
            f[n + 1][x + EX, c, h, ROWS, :] = 0.5 * (f[n - 1][x + EX, c, h, ROWS, :] + cen[c]) + 0.5 * wave_step * r[c]

    def smooth(n, x, h):
        src = f[n]
        for q, c in enumerate(ORDER):
            cen = src[x + EX, c, h, ROWS, :]
            nxt, prv = beside(n, x, c, h)
            total = (1.0 - filter_weight * 3.0 * filter_taps[0]) * cen
            for j in (1, 2, 3):
                t = ((src[x + EX + j, c, h, ROWS, :] + src[x + EX - j, c, h, ROWS, :])
                     + (src[x + EX, c, h, pl.ds(R0 + j, NY), :] + src[x + EX, c, h, pl.ds(R0 - j, NY), :])
                     + (ahead(cen, nxt, j) + behind(cen, prv, j)))
                total = total - (filter_weight * filter_taps[j]) * t
            if n + 1 == STAGES:
                stage[pl.ds(x * 128 + h * 4 + q, NY, stride=8), :] = total
            else:
                f[n + 1][x + EX, c, h, ROWS, :] = total

    def correct_rows(n, x):
        kind = n % 3
        taps = [filter_weight * w for w in filter_taps[1:]] if kind == 2 else derivative_weights
        w = wave_step if kind == 0 else 0.5 * wave_step

        def side_of(low):
            own = 0 if low else 8
            for h in range(2):
                for c in range(4) if kind == 2 else (QV, QP):
                    total = None
                    for j in (1, 2, 3):
                        p = taps[j - 1] * yh[n][x, c, h, pl.ds(8 - j if low else j, 8), :]
                        total = p if total is None else total + p
                    to = c if kind == 2 else QP + QV - c
                    if n + 1 == STAGES:
                        at = pl.ds(x * 128 + own * 8 + h * 4 + ORDER.index(c), 8, stride=8)
                        stage[at, :] = stage[at, :] - total
                    else:
                        at = pl.ds(R0 + own, 8)
                        change = total if kind == 2 else (-w if low else w) * total
                        f[n + 1][x + EX, to, h, at, :] = f[n + 1][x + EX, to, h, at, :] - change

        pl.when(iy == 1)(lambda: side_of(True))
        pl.when(iy == 0)(lambda: side_of(False))

    def correct(n, h):
        kind = n % 3
        taps = [filter_weight * w for w in filter_taps[1:]] if kind == 2 else derivative_weights

        def side_of(low):
            halo = [[xh[n][0 if low else 1, EX - k if low else k - 1, c, h] for c in range(4)] for k in (1, 2, 3)]
            for i in range(EX):
                x = i if low else NA - 1 - i
                d = []
                for c in range(4):
                    total = taps[i] * halo[0][c]
                    for k in range(1, EX - i):
                        total = total + taps[i + k] * halo[k][c]
                    d.append(total)
                if kind == 2:
                    change = d
                else:
                    w = (wave_step if kind == 0 else 0.5 * wave_step) * (-1.0 if low else 1.0)
                    m = w * mb[x]
                    change = [None] * 4
                    change[QP] = m * d[QP] + w * d[QU]
                    change[QU] = m * d[QU] + w * d[QP]
                    change[QV] = m * d[QV]
                    change[QW] = m * d[QW]
                for q, c in enumerate(ORDER):
                    if n + 1 == STAGES:
                        at = pl.ds(x * 128 + h * 4 + q, NY, stride=8)
                        stage[at, :] = stage[at, :] - change[c]
                    else:
                        f[n + 1][x + EX, c, h, ROWS, :] = f[n + 1][x + EX, c, h, ROWS, :] - change[c]

        pl.when(has_l)(lambda: side_of(True))
        pl.when(has_r)(lambda: side_of(False))

    def over(lo, hi, step):
        def go(x, _):
            step(lo + 2 * x)
            step(lo + 2 * x + 1)
            return 0
        lax.fori_loop(0, (hi - lo) // 2, go, 0)

    def both(step):
        def go(x):
            step(x, 0)
            step(x, 1)
        return go

    def rim(width, step):
        def go(i):
            step(jnp.where(i < width, i, i + NA - 2 * width))
        over(0, 2 * width, go)

    def mend(k):
        n = 3 * k + 1
        for h in range(2):
            terms[k][h].wait()

            def go(i):
                for c, q in enumerate((QU, QV, QW)):
                    for x0, slot in ((0, 0), (12, 1)):
                        f[n][x0 + i + EX, q, h, ROWS, :] = f[n][x0 + i + EX, q, h, ROWS, :] - wave_step * tb[k][slot, h, i, c]
            over(0, 4, go)
        cross[n][1].start()
        cross[n][2].start()
        for h in range(2):
            attach(k, h)

    def mend_halo(k, h):
        n = 3 * k + 1
        for low, slot, first_layer in ((0, 2, 1), (1, 3, 0)):
            def go():
                for j in range(EX):
                    for c, q in enumerate((QU, QV, QW)):
                        xh[n][low, j, q, h] = xh[n][low, j, q, h] - wave_step * tb[k][slot, h, j + first_layer, c]
            pl.when(has_r if low else has_l)(go)

    veils[0][1].wait()
    over(1, NX - 1, functools.partial(eddy, 0))
    veils[0][0].wait()
    over(0, 2, lambda i: eddy(0, i * (NX - 1)))
    for h in range(2):
        rim_terms(0, h)
        terms[0][h].start()
    own_terms(0)

    for n in range(STAGES):
        step = (functools.partial(first, n, n // 3), functools.partial(second, n, n // 3), functools.partial(smooth, n))[n % 3]
        if n == 2:
            for c in veils[1]:
                c.wait()
            over(0, NX, functools.partial(eddy, 1))
            rim_terms(1, 0)
            terms[1][0].start()
            rim_terms(1, 1)
            own_terms(1)
        cross[n][0].wait_twin()
        if n == 0:
            over(0, NA, both(step))
        else:
            width = 4 if n % 3 == 1 else EX
            over(width, NA - width, both(step))
            cross[n][1].wait_twin()
            cross[n][2].wait_twin()
            rim(width, lambda x: both(step)(x))
        cross[n][0].wait_side()
        if n % 3 == 2:
            over(EX, NA - EX, functools.partial(correct_rows, n))
            if n + 1 == STAGES:
                inner = pltpu.make_async_copy(stage.at[pl.ds(3 * 128, 10 * 128)], out.at[pl.ds(3 * 128, 10 * 128)], local.at[0])
                inner.start()
            else:
                cross[n + 1][0].start()
        for c in cross[n][1:]:
            c.wait_side()
        if n % 3 == 2:
            rim(EX, functools.partial(correct_rows, n))
        else:
            over(0, NA, functools.partial(correct_rows, n))
        if n % 3 == 1:
            cross[n + 1][0].start()
        for h in range(2):
            sides[n][h].wait()
            if n % 3 == 1:
                mend_halo(n // 3, h)
            correct(n, h)
            if n % 3 == 0:
                for j in range(EX):
                    for c in range(4):
                        sb[n // 3][0, j, c, h] = f[n + 1][EX + NA - EX + j, c, h, ROWS, :]
                        sb[n // 3][1, j, c, h] = f[n + 1][EX + j, c, h, ROWS, :]
            if n + 1 < STAGES:
                pl.when(sooner)(sides[n + 1][h].start)
        if n % 3 == 0:
            cross[n + 1][0].start()
        elif n + 1 < STAGES:
            cross[n + 1][1].start()
            cross[n + 1][2].start()
        if n + 1 < STAGES:
            @pl.when(later)
            def _():
                cross[n + 1][0 if n % 3 == 0 else 2].hear()
                for h in range(2):
                    sides[n + 1][h].start()
        if n % 3 == 0:
            mend(n // 3)
        if n == 0:
            for c in veils[1]:
                c.start()
        if n == 2:
            terms[1][1].start()
    outer = [pltpu.make_async_copy(stage.at[pl.ds(x * 128, 3 * 128)], out.at[pl.ds(x * 128, 3 * 128)], local.at[k])
             for k, x in ((1, 0), (2, 13))]
    for c in outer:
        c.start()
    for c in sent:
        c.drain()
    inner.wait()
    for c in outer:
        c.wait()


def solution(mesh):
    count = mesh.shape["gx"]
    placed = (
        P("gx", "gy", None, "grp"),
        P("gx", "gy"),
        P("gx", "gy", None, None, None),
        P("gx"),
        P("gx", "gy", None, "grp"),
    )

    def body(les_velocity, mean_mach, transfer_tiles, intersection_offset, acoustic_state):
        les = les_velocity.transpose(0, 2, 1, 3)
        state = acoustic_state.reshape(NA, NY, 4, 2, L).transpose(0, 1, 3, 2, 4).reshape(NA * NY * 8, L)
        anywhere = pl.BlockSpec(memory_space=pl.ANY)
        result = pl.pallas_call(
            functools.partial(kernel, count),
            out_shape=jax.ShapeDtypeStruct(state.shape, F32),
            in_specs=[anywhere, anywhere, anywhere, pl.BlockSpec(memory_space=pltpu.SMEM), anywhere],
            out_specs=anywhere,
            scratch_shapes=[
                pltpu.VMEM((NX + 2, 3, 2, 32, L), F32),
                pltpu.VMEM((NX + 2, 3, 2, 32, L), F32),
                pltpu.VMEM((NX, 3, NY, L), F32),
                pltpu.VMEM((NX, 3, NY, L), F32),
                *[pltpu.VMEM((NA + 2 * EX, 4, 2, 32, L), F32)] * STAGES,
                *[pltpu.VMEM((NA, 4, NY, L), F32)] * STAGES,
                *[pltpu.VMEM((2, EX, 4, 2, NY, L), F32)] * STAGES,
                *[pltpu.VMEM((NA, 4, 2, NY, L), F32)] * STAGES,
                *[pltpu.VMEM((2, EX, 4, 2, NY, L), F32)] * 2,
                *[pltpu.VMEM((NA, 3, 2, NY, L), F32)] * 2,
                *[pltpu.VMEM((4, 2, 4, 3, NY, L), F32)] * 2,
                pltpu.VMEM((NA * NY * 8 + 8, L), F32),
                pltpu.VMEM((8 * 128, 6 * L), BF16),
                pltpu.VMEM((6, 768, 64), BF16),
                pltpu.VMEM((NA, NY, L), F32),
                pltpu.VMEM((8, 2, 64, 64), BF16),
                pltpu.VMEM((NA, NY), F32),
                pltpu.SemaphoreType.DMA((72,)),
                pltpu.SemaphoreType.DMA((72,)),
                pltpu.SemaphoreType.DMA((8,)),
            ],
            compiler_params=pltpu.CompilerParams(collective_id=0, has_side_effects=True, vmem_limit_bytes=60 << 20),
        )(les, mean_mach, transfer_tiles[:, 0], intersection_offset, state)
        return result.reshape(NA, NY, 2, 4, L).transpose(0, 1, 3, 2, 4).reshape(acoustic_state.shape)

    return jax.shard_map(body, mesh=mesh, in_specs=placed, out_specs=P("gx", "gy", None, "grp"), check_vma=False)
```
